32 devices in a mesh: row: 4 (over y, x), col: 4 (over z), depth: 2 (over core).
Axes of the slice: x: 2, y: 2, z: 4, core: 2. Of those that a mesh axis runs over, the one named last changes fastest.
Arguments:
- a_band: bfloat16 [32, 16, 128, 128], P(('row', 'col'))
- a_fill: int32 [32, 16], P(('row', 'col')), may hold values from 0 to 1, as said below
- c_reach: int32 [32], P(('row', 'col')), may hold values from 16 to 24
Outputs:
- squared: bfloat16 [32, 24, 128, 128], P(('row', 'col'), None, 'depth')
The draws below stay inside these ranges and needn't reach their ends.
Inputs may be any that keep to these rules, and one draw needn't show every extreme that they name: a_fill[i, e] is 0 where i + e >= 32; it is 1 where e = 0 and where e = 15 and i + e < 32.
All inputs are finite; a program needn't handle non-finite values.
Results may differ from the reference program's by a relative error of at most 0.0045.
Values may be sent and summed in bfloat16 or wider, within the bound.
No kernel may reach another device: no remote copies, remote signals or barrier semaphores. Data moves between devices by JAX's collectives and lax.ppermute only.
A program may use at most 64 MiB of HBM per device.

```python
import jax
import jax.numpy as jnp
from jax import lax

TILE = 128
BAND = 16
OUT_BAND = 24
NB = 32


def draw_a_band(key, part):
    factor = float(BAND * TILE // 4) ** (-0.25)
    entries = jax.random.normal(key, (NB, BAND, TILE, TILE), jnp.float32)
    return (entries * factor).astype(jnp.bfloat16)


def draw_a_fill(key, part):
    row_index = jnp.arange(NB, dtype=jnp.int32)[:, None]
    band_index = jnp.arange(BAND, dtype=jnp.int32)[None, :]
    coin_flips = jax.random.randint(key, (NB, BAND), 0, 2, dtype=jnp.int32)
    inside = row_index + band_index < NB
    forced = (band_index == 0) | (band_index == BAND - 1)
    return jnp.where(inside & (forced | (coin_flips == 1)), 1, 0).astype(jnp.int32)


def plant(result, rng, least, largest):
    dims = result.shape
    index_at = [jax.random.randint(jax.random.fold_in(rng, axis), (), 0, dims[axis]) for axis in range(len(dims))]
    result = result.at[tuple(index_at)].set(least)
    longest = dims.index(max(dims))
    index_at[longest] = (index_at[longest] + 1) % dims[longest]
    return result.at[tuple(index_at)].set(largest)


def setup_inputs(seed: int = 0) -> dict:
    seeds = jax.random.split(jax.random.key(seed), 4)
    a_band = draw_a_band(jax.random.fold_in(seeds[3], 71), 0)
    a_fill = draw_a_fill(jax.random.fold_in(seeds[3], 71), 0)
    c_reach = plant(jax.random.randint(seeds[2], (NB,), BAND, OUT_BAND + 1), jax.random.fold_in(seeds[2], 1), BAND, OUT_BAND).astype(jnp.int32)
    return dict(a_band=a_band, a_fill=a_fill, c_reach=c_reach)


def reference(a_band, a_fill, c_reach):
    half_band = BAND // 2
    masked = a_band * a_fill.astype(jnp.bfloat16)[:, :, None, None]
    padded = jnp.concatenate([masked, jnp.zeros((BAND, BAND, TILE, TILE), jnp.bfloat16)], axis=0)

    def one_row(row_number):
        below = lax.dynamic_slice_in_dim(padded, row_number, BAND, 0).astype(jnp.float32)
        near_sum = jnp.zeros((2 * BAND, TILE, TILE), jnp.float32)
        far_sum = jnp.zeros((2 * BAND, TILE, TILE), jnp.float32)
        for k_offset in range(BAND):
            product_term = jnp.einsum("ab,ebc->eac", below[0, k_offset], below[k_offset], precision=lax.Precision.HIGHEST, preferred_element_type=jnp.float32)
            if k_offset < half_band:
                near_sum = near_sum.at[k_offset:k_offset + BAND].add(product_term)
            else:
                far_sum = far_sum.at[k_offset:k_offset + BAND].add(product_term)
        near_part = lax.optimization_barrier(near_sum[:OUT_BAND].astype(jnp.bfloat16))
        far_part = lax.optimization_barrier(far_sum[:OUT_BAND].astype(jnp.bfloat16))
        return near_part.astype(jnp.float32) + far_part.astype(jnp.float32)

    product = lax.map(one_row, jnp.arange(NB, dtype=jnp.int32))
    keep_tiles = jnp.arange(OUT_BAND, dtype=jnp.int32)[None, :] < c_reach[:, None]
    kept = jnp.where(keep_tiles[:, :, None, None], product, jnp.float32(0.0))
    return kept.astype(jnp.bfloat16)
```

```python
import functools

import jax
import jax.numpy as jnp
import numpy as np
from jax import lax
from jax.experimental import pallas as pl
from jax.experimental.pallas import tpu as pltpu
from jax.sharding import PartitionSpec as P

OUT_BAND = 24
TILE = 128
SLOTS = 8
SUMS = 16
NO_TERM = 17
RC = ("row", "col")


STEPS = (
    (1, (
        (1, 1, 1), (3, 3, 0), (4, 4, 1), (5, 5, 0), (6, 6, 0), (7, 7, 0), (8, 8, 0), (9, 9, 0),
        (10, 10, 0), (11, 11, 0), (12, 12, 0), (13, 13, 0), (14, 14, 0), (15, 15, 0),
    )),
    (0, (
        (4, 4, 0), (5, 5, 0), (6, 6, 1), (7, 7, 1), (8, 8, 1), (9, 9, 1), (10, 10, 0),
        (11, 11, 1), (12, 12, 0), (13, 13, 0), (14, 14, 0), (15, 15, 0),
    )),
    (5, (
        (2, 2, 1), (5, 5, 0), (6, 6, 0), (8, 8, 0), (9, 9, 0), (10, 10, 1), (11, 11, 1),
        (12, 12, 0), (13, 13, 0), (14, 14, 0), (15, 15, 0),
    )),
    (1, (
        (1, 1, 0), (3, 3, 1), (4, 4, 0), (5, 5, 1), (6, 6, 1), (7, 7, 1), (8, 8, 1), (9, 9, 1),
        (10, 10, 1), (11, 11, 1),
    )),
    (0, (
        (4, 4, 1), (5, 4, 1), (6, 7, 0), (7, 7, 0), (8, 9, 0), (9, 8, 0), (10, 11, 0),
        (11, 11, 0), (12, 13, 0), (13, 12, 0), (14, 15, 0), (15, 14, 0),
    )),
    (6, (
        (1, 9, 0), (2, 6, 1), (4, 5, 0), (5, 5, 1), (6, 7, 0), (8, 8, 1), (9, 9, 1),
        (10, 2, 1), (11, 10, 0), (12, 8, 1), (13, 9, 1), (14, 10, 0), (15, 11, 1),
    )),
    (1, (
        (0, 8, 0), (1, 5, 0), (2, 6, 1), (3, 7, 1), (4, 12, 0), (5, 6, 0), (6, 5, 0),
        (13, 14, 0), (14, 13, 0),
    )),
    (0, (
        (0, 8, 0), (2, 10, 1), (4, 5, 1), (5, 5, 1), (6, 6, 0), (7, 6, 0), (8, 9, 1),
        (11, 10, 1), (13, 14, 0), (14, 13, 0),
    )),
    (6, (
        (1, 4, 1), (2, 3, 1), (5, 4, 0), (6, 7, 1), (8, 13, 0), (9, 8, 1), (10, 10, 1),
        (11, 11, 0), (12, 9, 0), (13, 8, 0), (14, 11, 0), (15, 14, 0),
    )),
    (1, (
        (0, 8, 1), (1, 6, 1), (2, 9, 0), (3, 10, 0), (4, 8, 1), (5, 7, 0), (6, 5, 1),
        (7, 11, 1), (9, 2, 1), (10, 9, 1), (13, 10, 0), (14, 9, 1),
    )),
    (0, (
        (1, 6, 1), (2, 9, 0), (3, 10, 0), (4, 6, 0), (6, 5, 1), (7, 5, 0), (12, 14, 0),
        (13, 10, 0), (15, 13, 0),
    )),
    (6, (
        (1, 8, 0), (2, 2, 0), (5, 12, 0), (6, 10, 1), (10, 15, 0), (12, 9, 1), (14, 15, 0),
        (15, 13, 0),
    )),
    (1, (
        (0, 13, 0), (1, 3, 1), (2, 4, 1), (3, 11, 0), (4, 9, 0), (5, 7, 1), (6, 10, 1),
        (7, 14, 0), (9, 10, 1), (10, 8, 1), (13, 11, 0), (14, 8, 0),
    )),
    (0, (
        (1, 8, 0), (2, 10, 0), (3, 9, 0), (4, 7, 0), (5, 7, 1), (6, 4, 0), (7, 5, 1),
        (12, 10, 0),
    )),
    (6, (
        (2, 3, 0), (5, 8, 1), (6, 11, 1), (8, 2, 1), (9, 12, 0), (10, 11, 1), (11, 9, 1),
        (12, 10, 0), (15, 9, 1),
    )),
    (1, (
        (0, 6, 0), (1, 2, 0), (2, 8, 0), (4, 9, 1), (5, 10, 1), (6, 12, 0), (7, 13, 0),
        (9, 15, 0), (13, 15, 0),
    )),
    (0, (
        (0, 6, 1), (1, 13, 0), (2, 11, 0), (3, 11, 0), (4, 7, 1), (5, 7, 0), (6, 5, 0),
        (7, 10, 1), (12, 11, 0), (13, 11, 0),
    )),
    (4, (
        (1, 8, 1), (2, 4, 0), (11, 8, 1), (12, 11, 0), (13, 11, 0), (14, 8, 0), (15, 8, 0),
    )),
    (1, (
        (0, 2, 1), (1, 3, 0), (2, 4, 0), (3, 9, 1), (4, 10, 0), (5, 11, 1), (6, 8, 1),
        (7, 9, 1), (9, 11, 1), (10, 12, 0),
    )),
)
GROUPS = [0, 8, 13, 17, 19]


def partner(kind, chip):
    z, row = chip % 4, chip // 4
    if kind < 3:
        return chip ^ (4, 1, 8)[kind]
    if z in (1, 2) and (kind - 3) >> (row % 2) & 1:
        return chip ^ 3
    return chip ^ 8


def grid_plan():
    ops = []
    for kind, sends in STEPS:
        sent = {source: (block, part) for source, block, part in sends}
        ops.append([(c, partner(kind, c), sent.get(c)) for c in range(16)])
    groups = [["n0", "n1"]]
    groups += [list(range(a, b)) for a, b in zip(GROUPS, GROUPS[1:])]
    return ops, groups, frozenset(range(12, 16))

def direct_plan(chips):
    ops, groups = [], [["n0", "n1"]]
    for m in range(1, 9):
        for part in range(2 if m < 8 else 1):
            ops.append([(r + m, r, (r + m, part)) for r in range(chips - m)])
        if m % 3 == 0:
            groups.append([])
        if m == 1:
            groups.append([])
        groups[-1] += list(range(len(ops) - (2 if m < 8 else 1), len(ops)))
    return ops, groups, frozenset()


def first_slot(k, core):
    return (k - core + ((core + k) & 1)) // 2


def terms(block, part, chip, packed, core):
    m = block - chip
    if packed:
        ks = [2 * m, 2 * m + 1] if part == 0 else [NO_TERM, NO_TERM]
        at = [first_slot(k, core) for k in ks]
    else:
        ks = [2 * m + part] * 2
        at = [first_slot(ks[0], core), first_slot(ks[0], core) + SLOTS // 2]
    out = []
    for k, slot in zip(ks, at):
        out += [k, slot] if m >= 0 and k < NO_TERM else [NO_TERM, 0]
    return out


def select(index, choices):
    value = choices[-1]
    for i in reversed(range(len(choices) - 1)):
        value = jnp.where(index == i, choices[i], value)
    return value


VMEM = pl.BlockSpec(memory_space=pltpu.VMEM)
SMEM = pl.BlockSpec(memory_space=pltpu.SMEM)


def units_kernel(where_ref, fill_ref, band_ref, *unit_refs):
    for part, unit in enumerate(unit_refs):
        for slot in range(SLOTS):
            at = (part * SLOTS + slot) * 2
            row, entry = where_ref[at], where_ref[at + 1]
            fill = fill_ref[row, entry].astype(jnp.float32)
            tile = band_ref[row, entry].astype(jnp.float32) * fill
            unit[:, slot * TILE : (slot + 1) * TILE] = tile.astype(jnp.bfloat16)


def add_terms(table_ref, base, left_ref, units, sums):
    for i, unit in enumerate(units):
        for half in range(2):
            at = (base + i) * 4 + half * 2
            k, slot = table_ref[at], table_ref[at + 1]

            @pl.when(k < NO_TERM)
            def _(k=k, slot=slot, unit=unit, half=half):
                width = SLOTS // 2 * TILE
                product = jnp.dot(
                    left_ref[k],
                    unit[:, half * width : (half + 1) * width],
                    preferred_element_type=jnp.float32,
                )
                for q in range(SLOTS // 2):
                    sums[slot + q] += product[:, q * TILE : (q + 1) * TILE]


def first_kernel(base, table_ref, fill_ref, band_ref, *refs):
    units, (left, sums) = refs[:-2], refs[-2:]
    zero = jnp.zeros((TILE, TILE), jnp.bfloat16)
    left[0, TILE:] = zero
    left[16, :TILE] = zero
    for row in range(2):
        for entry in range(16):
            fill = fill_ref[row, entry].astype(jnp.float32)
            tile = band_ref[row, entry].astype(jnp.float32) * fill
            left[entry + row, row * TILE : (row + 1) * TILE] = tile.astype(jnp.bfloat16)
    sums[...] = jnp.zeros(sums.shape, jnp.float32)
    add_terms(table_ref, base, left, units, sums)


def more_kernel(base, table_ref, left_ref, *refs):
    units, sums_in, sums = refs[:-2], refs[-2], refs[-1]
    sums[...] = sums_in[...]
    add_terms(table_ref, base, left_ref, units, sums)


def last_kernel(base, table_ref, reach_ref, core_ref, left_ref, *refs):
    units, sums_in, kept, given, sums = refs[:-4], refs[-4], refs[-3], refs[-2], refs[-1]
    sums[...] = sums_in[...]
    add_terms(table_ref, base, left_ref, units, sums)
    core = core_ref[0]
    half = TILE // 2
    for row in range(2):
        odd = core if row == 0 else 1 - core
        shift = 0 if row == 0 else 1 - core
        for s in range(OUT_BAND // 2):
            keep = 2 * s + odd < reach_ref[row]
            for out, side in ((kept, core), (given, 1 - core)):
                start = pl.multiple_of(row * TILE + side * half, half)
                tile = sums[s + shift, pl.ds(start, half), :]
                out[row, s] = jnp.where(keep, tile, 0.0).astype(jnp.bfloat16)


def join_kernel(core_ref, kept_ref, taken_ref, out_ref):
    core = core_ref[0]
    for row in range(2):
        odd = core if row == 0 else 1 - core
        for s in range(OUT_BAND // 2):
            out_ref[row, 2 * s + odd] = kept_ref[row, s]
            out_ref[row, 2 * s + 1 - odd] = taken_ref[row, s]


def per_device(plan, chips, a_band, a_fill, c_reach):
    ops, groups, packed = plan
    core = lax.axis_index("depth")
    chip = lax.axis_index(RC)
    params = pltpu.CompilerParams(vmem_limit_bytes=48 * 2**20)

    where = np.zeros((chips, 2, 2, SLOTS, 2), np.int32)
    for r in range(chips):
        for c in range(2):
            for part in range(2):
                for t in range(SLOTS):
                    h = part
                    if r in packed and part == 0:
                        h = t // 4
                    e = t % 4 if r in packed and part == 0 else t
                    where[r, c, part, t] = (h, 2 * e + ((c + h) & 1))
    where = jnp.asarray(where.reshape(chips, 2, -1))[chip, core]

    held = {"n0": [(r, 0) for r in range(chips)], "n1": [(r, 1) for r in range(chips)]}
    picks = np.zeros((chips, max(1, len(ops))), np.int32)
    choices = []
    for o, moves in enumerate(ops):
        names = []
        got = [None] * chips
        for source, target, unit in moves:
            if unit is None:
                continue
            name = next(n for n, h in held.items() if h[source] == unit)
            if name not in names:
                names.append(name)
            picks[source, o] = names.index(name)
            got[target] = unit
        held[o] = got
        choices.append(names)
    order = [n for group in groups for n in group]
    table = np.full((chips, 2, len(order), 4), NO_TERM, np.int32)
    for r in range(chips):
        done = set()
        for i, n in enumerate(order):
            unit = held[n][r]
            if unit is None or unit in done:
                continue
            done.add(unit)
            for c in range(2):
                table[r, c, i] = terms(*unit, r, unit[0] in packed, c)
    table = jnp.asarray(table.reshape(chips, 2, -1))[chip, core]
    picks = jnp.asarray(picks)[chip]

    unit_shape = jax.ShapeDtypeStruct((TILE, SLOTS * TILE), jnp.bfloat16)
    sums_shape = jax.ShapeDtypeStruct((SUMS, 2 * TILE, TILE), jnp.float32)
    n0, n1 = pl.pallas_call(
        units_kernel,
        out_shape=(unit_shape, unit_shape),
        in_specs=[SMEM, SMEM, VMEM],
        out_specs=(VMEM, VMEM),
        compiler_params=params,
        name="units",
    )(where, a_fill, a_band)
    buffers = {"n0": n0, "n1": n1}
    for o, moves in enumerate(ops):
        payload = select(picks[o], [buffers[n] for n in choices[o]])
        buffers[o] = lax.ppermute(payload, RC, [(s, t) for s, t, _ in moves])

    core_arg = core.reshape(1).astype(jnp.int32)
    base = 0
    for g, group in enumerate(groups):
        units = [buffers[n] for n in group]
        if g == 0:
            left, sums = pl.pallas_call(
                functools.partial(first_kernel, base),
                out_shape=(jax.ShapeDtypeStruct((17, 2 * TILE, TILE), jnp.bfloat16), sums_shape),
                in_specs=[SMEM, SMEM, VMEM] + [VMEM] * len(units),
                out_specs=(VMEM, VMEM),
                compiler_params=params,
                name="first",
            )(table, a_fill, a_band, *units)
        elif g < len(groups) - 1:
            sums = pl.pallas_call(
                functools.partial(more_kernel, base),
                out_shape=sums_shape,
                in_specs=[SMEM, VMEM] + [VMEM] * (len(units) + 1),
                out_specs=VMEM,
                compiler_params=params,
                name="more",
            )(table, left, *units, sums)
        else:
            piece = jax.ShapeDtypeStruct((2, OUT_BAND // 2, TILE // 2, TILE), jnp.bfloat16)
            kept, given = pl.pallas_call(
                functools.partial(last_kernel, base),
                out_shape=(piece, piece),
                in_specs=[SMEM, SMEM, SMEM, VMEM] + [VMEM] * (len(units) + 1),
                out_specs=(VMEM, VMEM),
                scratch_shapes=[pltpu.VMEM(sums_shape.shape, jnp.float32)],
                compiler_params=params,
                name="last",
            )(table, c_reach, core_arg, left, *units, sums)
        base += len(group)
    taken = lax.ppermute(given, "depth", [(0, 1), (1, 0)])
    return pl.pallas_call(
        join_kernel,
        out_shape=jax.ShapeDtypeStruct((2, OUT_BAND, TILE // 2, TILE), jnp.bfloat16),
        in_specs=[SMEM, VMEM, VMEM],
        out_specs=VMEM,
        compiler_params=params,
        name="join",
    )(core_arg, kept, taken)


def solution(mesh):
    rows, cols = mesh.shape["row"], mesh.shape["col"]
    plan = grid_plan() if (rows, cols) == (4, 4) else direct_plan(rows * cols)
    in_specs = (P(RC, None, None, None), P(RC, None), P(RC))
    out_specs = P(RC, None, "depth", None)
    return jax.shard_map(
        functools.partial(per_device, plan, rows * cols),
        mesh=mesh,
        in_specs=in_specs,
        out_specs=out_specs,
        check_vma=False,
    )
```

```python
import functools

import jax
import jax.numpy as jnp
import numpy as np
from jax import lax
from jax.experimental import pallas as pl
from jax.experimental.pallas import tpu as pltpu
from jax.sharding import PartitionSpec as P

OUT_BAND = 24
TILE = 128
SLOTS = 8
SUMS = 16
NO_TERM = 17
RC = ("row", "col")


STEPS = (
    (1, (
        (1, 1, 1), (3, 3, 1), (4, 4, 0), (5, 5, 1), (7, 7, 1), (8, 8, 1), (9, 9, 1),
        (10, 10, 1), (11, 11, 0), (12, 12, 0), (13, 13, 0), (14, 14, 0), (15, 15, 0),
    )),
    (0, (
        (2, 2, 1), (4, 4, 1), (5, 5, 0), (6, 6, 0), (7, 7, 0), (8, 8, 0), (9, 9, 0),
        (10, 10, 1), (11, 11, 1), (12, 12, 0), (13, 13, 0), (14, 14, 0), (15, 15, 0),
    )),
    (5, (
        (2, 2, 1), (5, 5, 1), (6, 6, 1), (8, 8, 1), (9, 9, 1), (10, 10, 0), (11, 11, 0),
        (12, 12, 0), (13, 13, 0), (14, 14, 0), (15, 15, 0),
    )),
    (1, (
        (1, 1, 0), (3, 3, 0), (4, 4, 1), (5, 5, 0), (6, 6, 1), (7, 7, 0), (8, 8, 0), (9, 9, 0),
        (11, 11, 1),
    )),
    (0, (
        (4, 5, 1), (5, 4, 0), (6, 7, 1), (7, 7, 1), (8, 9, 1), (9, 8, 1), (10, 10, 0),
        (11, 10, 1), (12, 13, 0), (13, 12, 0), (14, 15, 0), (15, 14, 0),
    )),
    (6, (
        (1, 5, 0), (2, 2, 0), (5, 4, 0), (6, 6, 0), (8, 9, 1), (9, 9, 0), (10, 11, 0),
        (11, 11, 1), (12, 8, 0), (13, 9, 0), (14, 10, 1), (15, 11, 1),
    )),
    (1, (
        (0, 8, 1), (1, 5, 0), (2, 6, 0), (3, 11, 0), (4, 12, 0), (5, 6, 1), (6, 5, 1),
        (13, 14, 0), (14, 13, 0),
    )),
    (0, (
        (0, 8, 1), (2, 10, 0), (3, 11, 0), (4, 4, 0), (5, 4, 1), (6, 7, 0), (7, 6, 1),
        (8, 9, 0),
    )),
    (6, (
        (1, 9, 1), (2, 7, 1), (6, 7, 0), (8, 8, 0), (9, 8, 0), (10, 2, 1), (11, 10, 1),
        (12, 13, 0), (13, 8, 1), (14, 10, 0), (15, 14, 0),
    )),
    (1, (
        (0, 5, 1), (1, 2, 0), (2, 5, 0), (4, 8, 0), (5, 6, 0), (6, 4, 0), (7, 11, 1),
        (9, 11, 0), (10, 9, 0), (13, 10, 1), (14, 9, 0),
    )),
    (0, (
        (0, 9, 1), (1, 8, 1), (2, 11, 0), (4, 6, 1), (5, 6, 0), (6, 4, 0), (7, 5, 1),
        (12, 14, 0),
    )),
    (6, (
        (1, 8, 1), (2, 3, 1), (5, 12, 0), (6, 10, 0), (8, 9, 0), (9, 12, 0), (10, 11, 1),
        (12, 9, 0), (14, 15, 0), (15, 13, 0),
    )),
    (1, (
        (0, 8, 0), (1, 7, 1), (2, 9, 1), (3, 10, 1), (4, 13, 0), (5, 7, 0), (6, 10, 0),
        (7, 14, 0), (9, 2, 1), (10, 8, 0), (13, 10, 0), (14, 8, 1),
    )),
    (0, (
        (1, 7, 1), (2, 9, 1), (3, 10, 1), (4, 6, 0), (5, 6, 1), (6, 6, 1), (7, 4, 0),
        (8, 11, 0), (9, 11, 0), (12, 10, 1), (13, 14, 0), (14, 13, 0),
    )),
    (6, (
        (1, 4, 1), (2, 3, 0), (5, 8, 0), (6, 11, 1), (10, 15, 0), (11, 9, 0), (12, 10, 1),
        (15, 9, 0),
    )),
    (1, (
        (0, 9, 0), (1, 3, 1), (2, 8, 1), (3, 5, 1), (4, 9, 0), (5, 10, 0), (6, 12, 0),
        (7, 13, 0), (9, 11, 1), (10, 12, 0),
    )),
    (0, (
        (0, 7, 1), (1, 9, 1), (2, 10, 1), (3, 9, 1), (4, 7, 0), (5, 7, 0), (7, 10, 0),
        (12, 10, 0), (13, 10, 1),
    )),
    (4, (
        (1, 8, 0), (2, 2, 1), (8, 2, 1), (10, 10, 0), (11, 8, 0), (12, 11, 0), (13, 11, 0),
        (14, 8, 1), (15, 8, 1),
    )),
    (1, (
        (1, 3, 0), (2, 4, 1), (3, 9, 0), (4, 10, 1), (5, 11, 1), (6, 8, 0), (7, 9, 0),
        (9, 15, 0), (10, 13, 0), (13, 15, 0),
    )),
)


def partner(kind, chip):
    z, row = chip % 4, chip // 4
    if kind < 3:
        return chip ^ (4, 1, 8)[kind]
    if z in (1, 2) and (kind - 3) >> (row % 2) & 1:
        return chip ^ 3
    return chip ^ 8


def grid_plan():
    ops = []
    for kind, sends in STEPS:
        sent = {source: (block, part) for source, block, part in sends}
        ops.append([(c, partner(kind, c), sent.get(c)) for c in range(16)])
    return ops, frozenset(range(12, 16))


def direct_plan(chips):
    ops = []
    for m in range(1, 9):
        for part in range(2 if m < 8 else 1):
            ops.append([(r + m, r, (r + m, part)) for r in range(chips - m)])
    return ops, frozenset()


def first_slot(k, core):
    return (k - core + ((core + k) & 1)) // 2


def terms(block, part, chip, packed, core):
    m = block - chip
    if packed:
        ks = [2 * m, 2 * m + 1] if part == 0 else [NO_TERM, NO_TERM]
        at = [first_slot(k, core) for k in ks]
    else:
        ks = [2 * m + part] * 2
        at = [first_slot(ks[0], core), first_slot(ks[0], core) + SLOTS // 2]
    out = []
    for k, slot in zip(ks, at):
        out += [k, slot] if m >= 0 and k < NO_TERM else [NO_TERM, 0]
    return out


VMEM = pl.BlockSpec(memory_space=pltpu.VMEM)
SMEM = pl.BlockSpec(memory_space=pltpu.SMEM)
HBM = pl.BlockSpec(memory_space=pltpu.HBM)
VMEM_LIMIT = 12 * 2**20
FIRST = 3
LAG = 5
LAST = 1


def units_kernel(packed_from, masks, fill_hbm, band_hbm, *refs):
    outs, (fill_ref, band_ref, sems) = refs[:-3], refs[-3:]
    fill_copy = pltpu.make_async_copy(fill_hbm, fill_ref, sems.at[0])
    band_copy = pltpu.make_async_copy(band_hbm, band_ref, sems.at[1])
    fill_copy.start()
    band_copy.start()
    core = lax.axis_index("depth")
    chip = lax.axis_index("row") * lax.axis_size("col") + lax.axis_index("col")
    packed = chip >= packed_from
    fill_copy.wait()
    band_copy.wait()
    parts = [0, 1] + [(mask >> chip) & 1 for mask in masks]
    for part, unit in zip(parts, outs):
        for slot in range(SLOTS):
            both = packed & (part == 0)
            row = jnp.where(both, slot // 4, part)
            entry = 2 * jnp.where(both, slot % 4, slot) + ((core + row) & 1)
            fill = fill_ref[row, entry].astype(jnp.float32)
            tile = band_ref[row, entry].astype(jnp.float32) * fill
            unit[:, slot * TILE : (slot + 1) * TILE] = tile.astype(jnp.bfloat16)


def add_terms(table_ref, base, left_ref, units, sums):
    width = SLOTS // 2 * TILE
    for i, unit in enumerate(units):
        for half in range(2):
            at = (base + i) * 4 + half * 2
            k, slot = table_ref[at], table_ref[at + 1]
            product = jnp.dot(
                left_ref[k],
                unit[:, half * width : (half + 1) * width],
                preferred_element_type=jnp.float32,
            )
            for q in range(SLOTS // 2):
                sums[slot + q] += product[:, q * TILE : (q + 1) * TILE]


def first_kernel(base, table_ref, fill_ref, band_ref, *refs):
    units, (left, sums) = refs[:-2], refs[-2:]
    zero = jnp.zeros((TILE, TILE), jnp.bfloat16)
    left[0, TILE:] = zero
    left[16, :TILE] = zero
    left[NO_TERM] = jnp.zeros((2 * TILE, TILE), jnp.bfloat16)
    for row in range(2):
        for entry in range(16):
            fill = fill_ref[row, entry].astype(jnp.float32)
            tile = band_ref[row, entry].astype(jnp.float32) * fill
            left[entry + row, row * TILE : (row + 1) * TILE] = tile.astype(jnp.bfloat16)
    sums[...] = jnp.zeros(sums.shape, jnp.float32)
    add_terms(table_ref, base, left, units, sums)


def step_kernel(base, picked, n_units, table_ref, left_ref, *refs):
    units, choices, outs = refs[:n_units], refs[n_units:-3 if picked is not None else -2], refs[-2:]
    sums = refs[-1]
    if picked is not None:
        out = refs[-2]
        index = table_ref[picked]
        for i, choice in enumerate(choices):

            @pl.when(index == i)
            def _(choice=choice):
                out[...] = choice[...]

    add_terms(table_ref, base, left_ref, units, sums)


def last_kernel(base, table_ref, reach_ref, left_ref, *refs):
    units, kept, given, sums = refs[:-4], refs[-3], refs[-2], refs[-1]
    add_terms(table_ref, base, left_ref, units, sums)
    core = lax.axis_index("depth")
    half = TILE // 2
    for row in range(2):
        odd = core if row == 0 else 1 - core
        shift = 0 if row == 0 else 1 - core
        for s in range(OUT_BAND // 2):
            keep = 2 * s + odd < reach_ref[row]
            for out, side in ((kept, core), (given, 1 - core)):
                start = pl.multiple_of(row * TILE + side * half, half)
                tile = sums[s + shift, pl.ds(start, half), :]
                out[row, s] = jnp.where(keep, tile, 0.0).astype(jnp.bfloat16)


def join_kernel(kept_ref, taken_ref, out_ref):
    core = lax.axis_index("depth")
    for row in range(2):
        odd = core if row == 0 else 1 - core
        for s in range(OUT_BAND // 2):
            out_ref[row, 2 * s + odd] = kept_ref[row, s]
            out_ref[row, 2 * s + 1 - odd] = taken_ref[row, s]


def lookup(plan, chips):
    ops, packed = plan
    held = {"n0": [(r, 0) for r in range(chips)], "n1": [(r, 1) for r in range(chips)]}
    order = ["n0", "n1"] + list(range(len(ops)))
    picks = np.zeros((chips, 2, len(ops)), np.int32)
    choices = []
    for o, moves in enumerate(ops):
        names = []
        got = [None] * chips
        for source, target, unit in moves:
            if unit is None:
                continue
            name = next(n for n in order if n in held and held[n][source] == unit)
            if name not in names:
                names.append(name)
            picks[source, :, o] = names.index(name)
            got[target] = unit
        held[o] = got
        choices.append(names)
    table = np.zeros((chips, 2, len(order), 4), np.int32)
    for r in range(chips):
        done = set()
        for i, n in enumerate(order):
            unit = held[n][r]
            fresh = unit is not None and unit not in done
            done.add(unit)
            for c in range(2):
                none = [NO_TERM, 0, NO_TERM, 0]
                table[r, c, i] = terms(*unit, r, unit[0] in packed, c) if fresh else none
    whole = np.concatenate([table.reshape(chips * 2, -1), picks.reshape(chips * 2, -1)], 1)
    return whole, table.shape[2] * 4, choices


def per_device(plan, chips, a_band, a_fill, c_reach):
    ops, packed = plan
    whole, picks_at, choices = lookup(plan, chips)
    device = lax.axis_index(RC + ("depth",))
    table = jnp.asarray(whole)[device]
    params = pltpu.CompilerParams(vmem_limit_bytes=VMEM_LIMIT)
    unit_shape = jax.ShapeDtypeStruct((TILE, SLOTS * TILE), jnp.bfloat16)
    sums_shape = jax.ShapeDtypeStruct((SUMS, 2 * TILE, TILE), jnp.float32)
    early = [o for o in range(len(ops)) if set(choices[o]) == {"n0", "n1"}]
    at = [choices[o].index("n1") for o in early]
    bits = whole[::2, picks_at:]
    masks = [sum(int(bits[r, o] == i) << r for r in range(chips)) for o, i in zip(early, at)]
    n0, n1, *sent = pl.pallas_call(
        functools.partial(units_kernel, min(packed, default=chips), masks),
        out_shape=(unit_shape,) * (2 + len(early)),
        in_specs=[HBM, HBM],
        out_specs=(VMEM,) * (2 + len(early)),
        scratch_shapes=[
            pltpu.SMEM(a_fill.shape, a_fill.dtype),
            pltpu.VMEM(a_band.shape, a_band.dtype),
            pltpu.SemaphoreType.DMA((2,)),
        ],
        compiler_params=params,
        name="units",
    )(a_fill, a_band)
    buffers = {"n0": n0, "n1": n1}
    left = sums = None
    added = 0

    def start():
        return pl.pallas_call(
            functools.partial(first_kernel, 0),
            out_shape=(
                jax.ShapeDtypeStruct((NO_TERM + 1, 2 * TILE, TILE), jnp.bfloat16),
                sums_shape,
            ),
            in_specs=[SMEM, SMEM, VMEM, VMEM, VMEM],
            out_specs=(VMEM, VMEM),
            compiler_params=params,
            name="first",
        )(table, a_fill, a_band, n0, n1)

    def step(sums, picked, sources, units, base):
        out_shape = ([unit_shape] if picked is not None else []) + [sums_shape]
        n_in = 2 + len(units) + len(sources)
        return pl.pallas_call(
            functools.partial(step_kernel, base, picked, len(units)),
            out_shape=out_shape,
            in_specs=[SMEM] + [VMEM] * n_in,
            out_specs=[VMEM] * len(out_shape),
            input_output_aliases={n_in: len(out_shape) - 1},
            compiler_params=params,
            name="step",
        )(table, left, *units, *sources, sums)

    for o, moves in enumerate(ops):
        sources = [buffers[n] for n in choices[o]]
        if o == FIRST:
            left, sums = start()
        ready = max(added, min(o - LAG, o))
        units = [buffers[n] for n in range(added, ready)]
        if o in early or len(sources) == 1:
            payload = sent[early.index(o)] if o in early else sources[0]
            if units and o >= FIRST:
                (sums,) = step(sums, None, [], units, 2 + added)
                added = ready
        else:
            payload, sums = step(sums, picks_at + o, sources, units, 2 + added)
            added = ready
        buffers[o] = lax.ppermute(payload, RC, [(s, t) for s, t, _ in moves])
    while added < len(ops) - LAST:
        (sums,) = step(sums, None, [], [buffers[added]], 2 + added)
        added += 1

    piece = jax.ShapeDtypeStruct((2, OUT_BAND // 2, TILE // 2, TILE), jnp.bfloat16)
    units = [buffers[n] for n in range(added, len(ops))]
    n_in = 3 + len(units)
    kept, given, _ = pl.pallas_call(
        functools.partial(last_kernel, 2 + added),
        out_shape=(piece, piece, sums_shape),
        in_specs=[SMEM, SMEM] + [VMEM] * (n_in - 1),
        out_specs=(VMEM, VMEM, VMEM),
        input_output_aliases={n_in: 2},
        compiler_params=params,
        name="last",
    )(table, c_reach, left, *units, sums)
    taken = lax.ppermute(given, "depth", [(0, 1), (1, 0)])
    return pl.pallas_call(
        join_kernel,
        out_shape=jax.ShapeDtypeStruct((2, OUT_BAND, TILE // 2, TILE), jnp.bfloat16),
        in_specs=[VMEM, VMEM],
        out_specs=VMEM,
        compiler_params=params,
        name="join",
    )(kept, taken)


def solution(mesh):
    rows, cols = mesh.shape["row"], mesh.shape["col"]
    plan = grid_plan() if (rows, cols) == (4, 4) else direct_plan(rows * cols)
    in_specs = (P(RC, None, None, None), P(RC, None), P(RC))
    out_specs = P(RC, None, "depth", None)
    return jax.shard_map(
        functools.partial(per_device, plan, rows * cols),
        mesh=mesh,
        in_specs=in_specs,
        out_specs=out_specs,
        check_vma=False,
    )
```

```python
import functools

import jax
import jax.numpy as jnp
import numpy as np
from jax import lax
from jax.experimental import pallas as pl
from jax.experimental.pallas import tpu as pltpu
from jax.sharding import PartitionSpec as P

OUT_BAND = 24
TILE = 128
SLOTS = 8
SUMS = 16
NO_TERM = 17
RC = ("row", "col")


STEPS = (
    (1, (
        (1, 1, 1), (3, 3, 1), (4, 4, 0), (5, 5, 1), (7, 7, 1), (8, 8, 1), (9, 9, 1),
        (10, 10, 1), (11, 11, 0), (12, 12, 0), (13, 13, 0), (14, 14, 0), (15, 15, 0),
    )),
    (0, (
        (2, 2, 1), (4, 4, 1), (5, 5, 0), (6, 6, 0), (7, 7, 0), (8, 8, 0), (9, 9, 0),
        (10, 10, 1), (11, 11, 1), (12, 12, 0), (13, 13, 0), (14, 14, 0), (15, 15, 0),
    )),
    (5, (
        (2, 2, 1), (5, 5, 1), (6, 6, 1), (8, 8, 1), (9, 9, 1), (10, 10, 0), (11, 11, 0),
        (12, 12, 0), (13, 13, 0), (14, 14, 0), (15, 15, 0),
    )),
    (1, (
        (1, 1, 0), (3, 3, 0), (4, 4, 1), (5, 5, 0), (6, 6, 1), (7, 7, 0), (8, 8, 0), (9, 9, 0),
        (11, 11, 1),
    )),
    (0, (
        (4, 5, 1), (5, 4, 0), (6, 7, 1), (7, 7, 1), (8, 9, 1), (9, 8, 1), (10, 10, 0),
        (11, 10, 1), (12, 13, 0), (13, 12, 0), (14, 15, 0), (15, 14, 0),
    )),
    (6, (
        (1, 5, 0), (2, 2, 0), (5, 4, 0), (6, 6, 0), (8, 9, 1), (9, 9, 0), (10, 11, 0),
        (11, 11, 1), (12, 8, 0), (13, 9, 0), (14, 10, 1), (15, 11, 1),
    )),
    (1, (
        (0, 8, 1), (1, 5, 0), (2, 6, 0), (3, 11, 0), (4, 12, 0), (5, 6, 1), (6, 5, 1),
        (13, 14, 0), (14, 13, 0),
    )),
    (0, (
        (0, 8, 1), (2, 10, 0), (3, 11, 0), (4, 4, 0), (5, 4, 1), (6, 7, 0), (7, 6, 1),
        (8, 9, 0),
    )),
    (6, (
        (1, 9, 1), (2, 7, 1), (6, 7, 0), (8, 8, 0), (9, 8, 0), (10, 2, 1), (11, 10, 1),
        (12, 13, 0), (13, 8, 1), (14, 10, 0), (15, 14, 0),
    )),
    (1, (
        (0, 5, 1), (1, 2, 0), (2, 5, 0), (4, 8, 0), (5, 6, 0), (6, 4, 0), (7, 11, 1),
        (9, 11, 0), (10, 9, 0), (13, 10, 1), (14, 9, 0),
    )),
    (0, (
        (0, 9, 1), (1, 8, 1), (2, 11, 0), (4, 6, 1), (5, 6, 0), (6, 4, 0), (7, 5, 1),
        (12, 14, 0),
    )),
    (6, (
        (1, 8, 1), (2, 3, 1), (5, 12, 0), (6, 10, 0), (8, 9, 0), (9, 12, 0), (10, 11, 1),
        (12, 9, 0), (14, 15, 0), (15, 13, 0),
    )),
    (1, (
        (0, 8, 0), (1, 7, 1), (2, 9, 1), (3, 10, 1), (4, 13, 0), (5, 7, 0), (6, 10, 0),
        (7, 14, 0), (9, 2, 1), (10, 8, 0), (13, 10, 0), (14, 8, 1),
    )),
    (0, (
        (1, 7, 1), (2, 9, 1), (3, 10, 1), (4, 6, 0), (5, 6, 1), (6, 6, 1), (7, 4, 0),
        (8, 11, 0), (9, 11, 0), (12, 10, 1), (13, 14, 0), (14, 13, 0),
    )),
    (6, (
        (1, 4, 1), (2, 3, 0), (5, 8, 0), (6, 11, 1), (10, 15, 0), (11, 9, 0), (12, 10, 1),
        (15, 9, 0),
    )),
    (1, (
        (0, 9, 0), (1, 3, 1), (2, 8, 1), (3, 5, 1), (4, 9, 0), (5, 10, 0), (6, 12, 0),
        (7, 13, 0), (9, 11, 1), (10, 12, 0),
    )),
    (0, (
        (0, 7, 1), (1, 9, 1), (2, 10, 1), (3, 9, 1), (4, 7, 0), (5, 7, 0), (7, 10, 0),
        (12, 10, 0), (13, 10, 1),
    )),
    (4, (
        (1, 8, 0), (2, 2, 1), (8, 2, 1), (10, 10, 0), (11, 8, 0), (12, 11, 0), (13, 11, 0),
        (14, 8, 1), (15, 8, 1),
    )),
    (1, (
        (1, 3, 0), (2, 4, 1), (3, 9, 0), (4, 10, 1), (5, 11, 1), (6, 8, 0), (7, 9, 0),
        (9, 15, 0), (10, 13, 0), (13, 15, 0),
    )),
)


def partner(kind, chip):
    z, row = chip % 4, chip // 4
    if kind < 3:
        return chip ^ (4, 1, 8)[kind]
    if z in (1, 2) and (kind - 3) >> (row % 2) & 1:
        return chip ^ 3
    return chip ^ 8


def grid_plan():
    ops = []
    for kind, sends in STEPS:
        sent = {source: (block, part) for source, block, part in sends}
        ops.append([(c, partner(kind, c), sent.get(c)) for c in range(16)])
    return ops, frozenset(range(12, 16))


def direct_plan(chips):
    ops = []
    for m in range(1, 9):
        for part in range(2 if m < 8 else 1):
            ops.append([(r + m, r, (r + m, part)) for r in range(chips - m)])
    return ops, frozenset()


def first_slot(k, core):
    return (k - core + ((core + k) & 1)) // 2


def terms(block, part, chip, packed, core):
    m = block - chip
    if packed:
        ks = [2 * m, 2 * m + 1] if part == 0 else [NO_TERM, NO_TERM]
        at = [first_slot(k, core) for k in ks]
    else:
        ks = [2 * m + part] * 2
        at = [first_slot(ks[0], core), first_slot(ks[0], core) + SLOTS // 2]
    out = []
    for k, slot in zip(ks, at):
        out += [k, slot] if m >= 0 and k < NO_TERM else [NO_TERM, 0]
    return out


VMEM = pl.BlockSpec(memory_space=pltpu.VMEM)
SMEM = pl.BlockSpec(memory_space=pltpu.SMEM)
HBM = pl.BlockSpec(memory_space=pltpu.HBM)
VMEM_LIMIT = 12 * 2**20
FIRST = 4
LAG = 4
ADD_AT = (8, 11, 14, 17)
LAST = (3, 1)


def units_kernel(packed_from, masks, choice_masks, fill_hbm, band_hbm, *refs):
    outs, flags, (fill_ref, band_ref, sems) = refs[:-4], refs[-4], refs[-3:]
    fill_copy = pltpu.make_async_copy(fill_hbm, fill_ref, sems.at[0])
    band_copy = pltpu.make_async_copy(band_hbm, band_ref, sems.at[1])
    fill_copy.start()
    band_copy.start()
    core = lax.axis_index("depth")
    chip = lax.axis_index("row") * lax.axis_size("col") + lax.axis_index("col")
    packed = chip >= packed_from
    fill_copy.wait()
    band_copy.wait()
    parts = [0, 1] + [(mask >> chip) & 1 for mask in masks]
    for part, unit in zip(parts, outs):
        for slot in range(SLOTS):
            both = packed & (part == 0)
            row = jnp.where(both, slot // 4, part)
            entry = 2 * jnp.where(both, slot % 4, slot) + ((core + row) & 1)
            fill = fill_ref[row, entry].astype(jnp.float32)
            tile = band_ref[row, entry].astype(jnp.float32) * fill
            unit[:, slot * TILE : (slot + 1) * TILE] = tile.astype(jnp.bfloat16)
    for i, mask in enumerate(choice_masks):
        bit = ((mask >> chip) & 1).astype(jnp.float32)
        flags[i : i + 1, :] = jnp.full((1, flags.shape[1]), bit, flags.dtype)


def add_terms(table_ref, base, left_ref, units, sums):
    width = SLOTS // 2 * TILE
    for i, unit in enumerate(units):
        for half in range(2):
            at = (base + i) * 4 + half * 2
            k, slot = table_ref[at], table_ref[at + 1]
            product = jnp.dot(
                left_ref[k],
                unit[:, half * width : (half + 1) * width],
                preferred_element_type=jnp.float32,
            )
            for q in range(SLOTS // 2):
                sums[slot + q] += product[:, q * TILE : (q + 1) * TILE]


def first_kernel(base, table_ref, fill_ref, band_ref, *refs):
    units, (left, token, sums) = refs[:-3], refs[-3:]
    token[...] = jnp.zeros(token.shape, token.dtype)
    zero = jnp.zeros((TILE, TILE), jnp.bfloat16)
    left[0, TILE:] = zero
    left[16, :TILE] = zero
    left[NO_TERM] = jnp.zeros((2 * TILE, TILE), jnp.bfloat16)
    for row in range(2):
        for entry in range(16):
            fill = fill_ref[row, entry].astype(jnp.float32)
            tile = band_ref[row, entry].astype(jnp.float32) * fill
            left[entry + row, row * TILE : (row + 1) * TILE] = tile.astype(jnp.bfloat16)
    sums[...] = jnp.zeros(sums.shape, jnp.float32)
    add_terms(table_ref, base, left, units, sums)


def more_kernel(base, table_ref, left_ref, after_ref, *refs):
    units, (token, sums) = refs[:-3], refs[-2:]
    token[...] = jnp.zeros(token.shape, token.dtype)
    add_terms(table_ref, base, left_ref, units, sums)


def last_kernel(base, table_ref, reach_ref, left_ref, *refs):
    units, kept, given, sums = refs[:-4], refs[-3], refs[-2], refs[-1]
    add_terms(table_ref, base, left_ref, units, sums)
    core = lax.axis_index("depth")
    half = TILE // 2
    for row in range(2):
        odd = core if row == 0 else 1 - core
        shift = 0 if row == 0 else 1 - core
        for s in range(OUT_BAND // 2):
            keep = 2 * s + odd < reach_ref[row]
            for out, side in ((kept, core), (given, 1 - core)):
                start = pl.multiple_of(row * TILE + side * half, half)
                tile = sums[s + shift, pl.ds(start, half), :]
                out[row, s] = jnp.where(keep, tile, 0.0).astype(jnp.bfloat16)


def join_kernel(kept_ref, taken_ref, out_ref):
    core = lax.axis_index("depth")
    for row in range(2):
        odd = core if row == 0 else 1 - core
        for s in range(OUT_BAND // 2):
            out_ref[row, 2 * s + odd] = kept_ref[row, s]
            out_ref[row, 2 * s + 1 - odd] = taken_ref[row, s]


def lookup(plan, chips):
    ops, packed = plan
    held = {"n0": [(r, 0) for r in range(chips)], "n1": [(r, 1) for r in range(chips)]}
    order = ["n0", "n1"] + list(range(len(ops)))
    picks = np.zeros((chips, len(ops)), np.int32)
    choices = []
    for o, moves in enumerate(ops):
        names = []
        got = [None] * chips
        for source, target, unit in moves:
            if unit is None:
                continue
            name = next(n for n in order if n in held and held[n][source] == unit)
            if name not in names:
                names.append(name)
            picks[source, o] = names.index(name)
            got[target] = unit
        held[o] = got
        choices.append(names)
    table = np.zeros((chips, 2, len(order), 4), np.int32)
    for r in range(chips):
        done = set()
        for i, n in enumerate(order):
            unit = held[n][r]
            fresh = unit is not None and unit not in done
            done.add(unit)
            for c in range(2):
                none = [NO_TERM, 0, NO_TERM, 0]
                table[r, c, i] = terms(*unit, r, unit[0] in packed, c) if fresh else none
    return table.reshape(chips * 2, -1), picks, choices


def per_device(plan, chips, a_band, a_fill, c_reach):
    ops, packed = plan
    table, picks, choices = lookup(plan, chips)
    table = jnp.asarray(table)[lax.axis_index(RC + ("depth",))]
    params = pltpu.CompilerParams(vmem_limit_bytes=VMEM_LIMIT)
    unit_shape = jax.ShapeDtypeStruct((TILE, SLOTS * TILE), jnp.bfloat16)
    token_shape = jax.ShapeDtypeStruct((1, SLOTS * TILE), jnp.float32)
    sums_shape = jax.ShapeDtypeStruct((SUMS, 2 * TILE, TILE), jnp.float32)
    early = [o for o in range(len(ops)) if set(choices[o]) == {"n0", "n1"}]
    at = [choices[o].index("n1") for o in early]
    masks = [sum(int(picks[r, o] == i) << r for r in range(chips)) for o, i in zip(early, at)]
    choice_masks, flag_at = [], {}
    for o, names in enumerate(choices):
        if o not in early:
            flag_at[o] = len(choice_masks)
            for i in range(len(names) - 1):
                choice_masks.append(sum(int(picks[r, o] == i) << r for r in range(chips)))
    flags_shape = jax.ShapeDtypeStruct((max(8, len(choice_masks)), SLOTS * TILE), jnp.float32)
    *sent, flags = pl.pallas_call(
        functools.partial(units_kernel, min(packed, default=chips), masks, choice_masks),
        out_shape=(unit_shape,) * (2 + len(early)) + (flags_shape,),
        in_specs=[HBM, HBM],
        out_specs=(VMEM,) * (3 + len(early)),
        scratch_shapes=[
            pltpu.SMEM(a_fill.shape, a_fill.dtype),
            pltpu.VMEM(a_band.shape, a_band.dtype),
            pltpu.SemaphoreType.DMA((2,)),
        ],
        compiler_params=params,
        name="units",
    )(a_fill, a_band)
    n0, n1, *sent = sent
    buffers = {"n0": n0, "n1": n1}
    payload = left = sums = None
    added = 0

    def start():
        return pl.pallas_call(
            functools.partial(first_kernel, 0),
            out_shape=(
                jax.ShapeDtypeStruct((NO_TERM + 1, 2 * TILE, TILE), jnp.bfloat16),
                token_shape,
                sums_shape,
            ),
            in_specs=[SMEM, SMEM, VMEM, VMEM, VMEM],
            out_specs=(VMEM, VMEM, VMEM),
            compiler_params=params,
            name="first",
        )(table, a_fill, a_band, n0, n1)

    def more(after, sums, units, base):
        return pl.pallas_call(
            functools.partial(more_kernel, base),
            out_shape=(token_shape, sums_shape),
            in_specs=[SMEM] + [VMEM] * (3 + len(units)),
            out_specs=(VMEM, VMEM),
            input_output_aliases={3 + len(units): 1},
            compiler_params=params,
            name="more",
        )(table, left, after, *units, sums)

    for o, moves in enumerate(ops):
        sources = [buffers[n] for n in choices[o]]
        if o in early:
            payload = sent[early.index(o)]
        else:
            order = 0 * payload[:1].astype(jnp.float32) if o > 0 else 0
            if o == FIRST:
                left, token, sums = start()
                order += token
            elif o in ADD_AT:
                units = [buffers[n] for n in range(added, o - LAG)]
                token, sums = more(payload, sums, units, 2 + added)
                added = o - LAG
                order += token
            payload = sources[-1]
            for i in reversed(range(len(sources) - 1)):
                at = flag_at[o] + i
                payload = jnp.where(flags[at : at + 1] + order > 0.5, sources[i], payload)
        buffers[o] = lax.ppermute(payload, RC, [(s, t) for s, t, _ in moves])
    if sums is None:
        left, _, sums = start()
    for count in LAST:
        units = [buffers[n] for n in range(added, len(ops) - count)]
        _, sums = more(units[0], sums, units, 2 + added)
        added += len(units)

    piece = jax.ShapeDtypeStruct((2, OUT_BAND // 2, TILE // 2, TILE), jnp.bfloat16)
    units = [buffers[n] for n in range(added, len(ops))]
    n_in = 3 + len(units)
    kept, given, _ = pl.pallas_call(
        functools.partial(last_kernel, 2 + added),
        out_shape=(piece, piece, sums_shape),
        in_specs=[SMEM, SMEM] + [VMEM] * (n_in - 1),
        out_specs=(VMEM, VMEM, VMEM),
        input_output_aliases={n_in: 2},
        compiler_params=params,
        name="last",
    )(table, c_reach, left, *units, sums)
    taken = lax.ppermute(given, "depth", [(0, 1), (1, 0)])
    return pl.pallas_call(
        join_kernel,
        out_shape=jax.ShapeDtypeStruct((2, OUT_BAND, TILE // 2, TILE), jnp.bfloat16),
        in_specs=[VMEM, VMEM],
        out_specs=VMEM,
        compiler_params=params,
        name="join",
    )(kept, taken)


def solution(mesh):
    rows, cols = mesh.shape["row"], mesh.shape["col"]
    plan = grid_plan() if (rows, cols) == (4, 4) else direct_plan(rows * cols)
    in_specs = (P(RC, None, None, None), P(RC, None), P(RC))
    out_specs = P(RC, None, "depth", None)
    return jax.shard_map(
        functools.partial(per_device, plan, rows * cols),
        mesh=mesh,
        in_specs=in_specs,
        out_specs=out_specs,
        check_vma=False,
    )
```

```python
import functools

import jax
import jax.numpy as jnp
import numpy as np
from jax import lax
from jax.experimental import pallas as pl
from jax.experimental.pallas import tpu as pltpu
from jax.sharding import PartitionSpec as P

OUT_BAND = 24
TILE = 128
SLOTS = 8
SUMS = 16
NO_TERM = 17
RC = ("row", "col")


STEPS = (
    (1, (
        (1, 1, 1), (3, 3, 1), (4, 4, 0), (5, 5, 1), (7, 7, 1), (8, 8, 1), (9, 9, 1),
        (10, 10, 1), (11, 11, 0), (12, 12, 0), (13, 13, 0), (14, 14, 0), (15, 15, 0),
    )),
    (0, (
        (2, 2, 1), (4, 4, 1), (5, 5, 0), (6, 6, 0), (7, 7, 0), (8, 8, 0), (9, 9, 0),
        (10, 10, 1), (11, 11, 1), (12, 12, 0), (13, 13, 0), (14, 14, 0), (15, 15, 0),
    )),
    (5, (
        (2, 2, 1), (5, 5, 1), (6, 6, 1), (8, 8, 1), (9, 9, 1), (10, 10, 0), (11, 11, 0),
        (12, 12, 0), (13, 13, 0), (14, 14, 0), (15, 15, 0),
    )),
    (1, (
        (1, 1, 0), (3, 3, 0), (4, 4, 1), (5, 5, 0), (6, 6, 1), (7, 7, 0), (8, 8, 0), (9, 9, 0),
        (11, 11, 1),
    )),
    (0, (
        (4, 5, 1), (5, 4, 0), (6, 7, 1), (7, 7, 1), (8, 9, 1), (9, 8, 1), (10, 10, 0),
        (11, 10, 1), (12, 13, 0), (13, 12, 0), (14, 15, 0), (15, 14, 0),
    )),
    (6, (
        (1, 5, 0), (2, 2, 0), (5, 4, 0), (6, 6, 0), (8, 9, 1), (9, 9, 0), (10, 11, 0),
        (11, 11, 1), (12, 8, 0), (13, 9, 0), (14, 10, 1), (15, 11, 1),
    )),
    (1, (
        (0, 8, 1), (1, 5, 0), (2, 6, 0), (3, 11, 0), (4, 12, 0), (5, 6, 1), (6, 5, 1),
        (13, 14, 0), (14, 13, 0),
    )),
    (0, (
        (0, 8, 1), (2, 10, 0), (3, 11, 0), (4, 4, 0), (5, 4, 1), (6, 7, 0), (7, 6, 1),
        (8, 9, 0),
    )),
    (6, (
        (1, 9, 1), (2, 7, 1), (6, 7, 0), (8, 8, 0), (9, 8, 0), (10, 2, 1), (11, 10, 1),
        (12, 13, 0), (13, 8, 1), (14, 10, 0), (15, 14, 0),
    )),
    (1, (
        (0, 5, 1), (1, 2, 0), (2, 5, 0), (4, 8, 0), (5, 6, 0), (6, 4, 0), (7, 11, 1),
        (9, 11, 0), (10, 9, 0), (13, 10, 1), (14, 9, 0),
    )),
    (0, (
        (0, 9, 1), (1, 8, 1), (2, 11, 0), (4, 6, 1), (5, 6, 0), (6, 4, 0), (7, 5, 1),
        (12, 14, 0),
    )),
    (6, (
        (1, 8, 1), (2, 3, 1), (5, 12, 0), (6, 10, 0), (8, 9, 0), (9, 12, 0), (10, 11, 1),
        (12, 9, 0), (14, 15, 0), (15, 13, 0),
    )),
    (1, (
        (0, 8, 0), (1, 7, 1), (2, 9, 1), (3, 10, 1), (4, 13, 0), (5, 7, 0), (6, 10, 0),
        (7, 14, 0), (9, 2, 1), (10, 8, 0), (13, 10, 0), (14, 8, 1),
    )),
    (0, (
        (1, 7, 1), (2, 9, 1), (3, 10, 1), (4, 6, 0), (5, 6, 1), (6, 6, 1), (7, 4, 0),
        (8, 11, 0), (9, 11, 0), (12, 10, 1), (13, 14, 0), (14, 13, 0),
    )),
    (6, (
        (1, 4, 1), (2, 3, 0), (5, 8, 0), (6, 11, 1), (10, 15, 0), (11, 9, 0), (12, 10, 1),
        (15, 9, 0),
    )),
    (1, (
        (0, 9, 0), (1, 3, 1), (2, 8, 1), (3, 5, 1), (4, 9, 0), (5, 10, 0), (6, 12, 0),
        (7, 13, 0), (9, 11, 1), (10, 12, 0),
    )),
    (0, (
        (0, 7, 1), (1, 9, 1), (2, 10, 1), (3, 9, 1), (4, 7, 0), (5, 7, 0), (7, 10, 0),
        (12, 10, 0), (13, 10, 1),
    )),
    (4, (
        (1, 8, 0), (2, 2, 1), (8, 2, 1), (10, 10, 0), (11, 8, 0), (12, 11, 0), (13, 11, 0),
        (14, 8, 1), (15, 8, 1),
    )),
    (1, (
        (1, 3, 0), (2, 4, 1), (3, 9, 0), (4, 10, 1), (5, 11, 1), (6, 8, 0), (7, 9, 0),
        (9, 15, 0), (10, 13, 0), (13, 15, 0),
    )),
)


def partner(kind, chip):
    z, row = chip % 4, chip // 4
    if kind < 3:
        return chip ^ (4, 1, 8)[kind]
    if z in (1, 2) and (kind - 3) >> (row % 2) & 1:
        return chip ^ 3
    return chip ^ 8


def grid_plan():
    ops = []
    for kind, sends in STEPS:
        sent = {source: (block, part) for source, block, part in sends}
        ops.append([(c, partner(kind, c), sent.get(c)) for c in range(16)])
    return ops, frozenset(range(12, 16))


def direct_plan(chips):
    ops = []
    for m in range(1, 9):
        for part in range(2 if m < 8 else 1):
            ops.append([(r + m, r, (r + m, part)) for r in range(chips - m)])
    return ops, frozenset()


def first_slot(k, core):
    return (k - core + ((core + k) & 1)) // 2


def terms(block, part, chip, packed, core):
    m = block - chip
    if packed:
        ks = [2 * m, 2 * m + 1] if part == 0 else [NO_TERM, NO_TERM]
        at = [first_slot(k, core) for k in ks]
    else:
        ks = [2 * m + part] * 2
        at = [first_slot(ks[0], core), first_slot(ks[0], core) + SLOTS // 2]
    out = []
    for k, slot in zip(ks, at):
        out += [k, slot] if m >= 0 and k < NO_TERM else [NO_TERM, 0]
    return out


VMEM = pl.BlockSpec(memory_space=pltpu.VMEM)
SMEM = pl.BlockSpec(memory_space=pltpu.SMEM)
HBM = pl.BlockSpec(memory_space=pltpu.HBM)
VMEM_LIMIT = 12 * 2**20
FIRST = 4
LAG = 4
ADD_AT = (8, 11, 14, 17)
LAST = (3, 1)


def units_kernel(packed_from, masks, choice_masks, fill_hbm, band_hbm, *refs):
    outs, flags, (fill_ref, band_ref, sems) = refs[:-4], refs[-4], refs[-3:]
    fill_copy = pltpu.make_async_copy(fill_hbm, fill_ref, sems.at[0])
    band_copy = pltpu.make_async_copy(band_hbm, band_ref, sems.at[1])
    fill_copy.start()
    band_copy.start()
    core = lax.axis_index("depth")
    chip = lax.axis_index("row") * lax.axis_size("col") + lax.axis_index("col")
    packed = chip >= packed_from
    fill_copy.wait()
    band_copy.wait()
    parts = [0, 1] + [(mask >> chip) & 1 for mask in masks]
    for part, unit in zip(parts, outs):
        for slot in range(SLOTS):
            both = packed & (part == 0)
            row = jnp.where(both, slot // 4, part)
            entry = 2 * jnp.where(both, slot % 4, slot) + ((core + row) & 1)
            fill = fill_ref[row, entry].astype(jnp.float32)
            tile = band_ref[row, entry].astype(jnp.float32) * fill
            unit[:, slot * TILE : (slot + 1) * TILE] = tile.astype(jnp.bfloat16)
    for i, mask in enumerate(choice_masks):
        bit = ((mask >> chip) & 1).astype(jnp.float32)
        flags[i : i + 1, :] = jnp.full((1, flags.shape[1]), bit, flags.dtype)


def add_terms(table_ref, base, left_ref, units, sums):
    width = SLOTS // 2 * TILE
    for i, unit in enumerate(units):
        for half in range(2):
            at = (base + i) * 4 + half * 2
            k, slot = table_ref[at], table_ref[at + 1]
            product = jnp.dot(
                left_ref[k],
                unit[:, half * width : (half + 1) * width],
                preferred_element_type=jnp.float32,
            )
            for q in range(SLOTS // 2):
                sums[slot + q] += product[:, q * TILE : (q + 1) * TILE]


def first_kernel(base, table_ref, fill_ref, band_ref, *refs):
    units, (left, token, sums) = refs[:-3], refs[-3:]
    token[...] = jnp.zeros(token.shape, token.dtype)
    zero = jnp.zeros((TILE, TILE), jnp.bfloat16)
    left[0, TILE:] = zero
    left[16, :TILE] = zero
    left[NO_TERM] = jnp.zeros((2 * TILE, TILE), jnp.bfloat16)
    for row in range(2):
        for entry in range(16):
            fill = fill_ref[row, entry].astype(jnp.float32)
            tile = band_ref[row, entry].astype(jnp.float32) * fill
            left[entry + row, row * TILE : (row + 1) * TILE] = tile.astype(jnp.bfloat16)
    sums[...] = jnp.zeros(sums.shape, jnp.float32)
    add_terms(table_ref, base, left, units, sums)


def more_kernel(base, table_ref, left_ref, after_ref, *refs):
    units, (token, sums) = refs[:-3], refs[-2:]
    token[...] = jnp.zeros(token.shape, token.dtype)
    add_terms(table_ref, base, left_ref, units, sums)


def last_kernel(base, table_ref, reach_ref, left_ref, *refs):
    units, kept, given, sums = refs[:-4], refs[-3], refs[-2], refs[-1]
    add_terms(table_ref, base, left_ref, units, sums)
    core = lax.axis_index("depth")
    half = TILE // 2
    for row in range(2):
        odd = core if row == 0 else 1 - core
        shift = 0 if row == 0 else 1 - core
        for s in range(OUT_BAND // 2):
            keep = 2 * s + odd < reach_ref[row]
            for out, side in ((kept, core), (given, 1 - core)):
                start = pl.multiple_of(row * TILE + side * half, half)
                tile = sums[s + shift, pl.ds(start, half), :]
                out[row, s] = jnp.where(keep, tile, 0.0).astype(jnp.bfloat16)


def join_kernel(kept_ref, taken_ref, out_ref):
    core = lax.axis_index("depth")
    for row in range(2):
        odd = core if row == 0 else 1 - core
        for s in range(OUT_BAND // 2):
            out_ref[row, 2 * s + odd] = kept_ref[row, s]
            out_ref[row, 2 * s + 1 - odd] = taken_ref[row, s]


def lookup(plan, chips):
    ops, packed = plan
    held = {"n0": [(r, 0) for r in range(chips)], "n1": [(r, 1) for r in range(chips)]}
    order = ["n0", "n1"] + list(range(len(ops)))
    picks = np.zeros((chips, len(ops)), np.int32)
    choices = []
    for o, moves in enumerate(ops):
        names = []
        got = [None] * chips
        for source, target, unit in moves:
            if unit is None:
                continue
            name = next(n for n in order if n in held and held[n][source] == unit)
            if name not in names:
                names.append(name)
            picks[source, o] = names.index(name)
            got[target] = unit
        held[o] = got
        choices.append(names)
    table = np.zeros((chips, 2, len(order), 4), np.int32)
    for r in range(chips):
        done = set()
        for i, n in enumerate(order):
            unit = held[n][r]
            fresh = unit is not None and unit not in done
            done.add(unit)
            for c in range(2):
                none = [NO_TERM, 0, NO_TERM, 0]
                table[r, c, i] = terms(*unit, r, unit[0] in packed, c) if fresh else none
    return table.reshape(chips * 2, -1), picks, choices


def per_device(plan, chips, a_band, a_fill, c_reach):
    ops, packed = plan
    table, picks, choices = lookup(plan, chips)
    table = jnp.asarray(table)[lax.axis_index(RC + ("depth",))]
    fill = pltpu.with_memory_space_constraint(a_fill, pltpu.HBM)
    band = pltpu.with_memory_space_constraint(a_band, pltpu.HBM)
    params = pltpu.CompilerParams(vmem_limit_bytes=VMEM_LIMIT)
    unit_shape = jax.ShapeDtypeStruct((TILE, SLOTS * TILE), jnp.bfloat16)
    token_shape = jax.ShapeDtypeStruct((1, SLOTS * TILE), jnp.float32)
    sums_shape = jax.ShapeDtypeStruct((SUMS, 2 * TILE, TILE), jnp.float32)
    early = [o for o in range(len(ops)) if set(choices[o]) == {"n0", "n1"}]
    at = [choices[o].index("n1") for o in early]
    masks = [sum(int(picks[r, o] == i) << r for r in range(chips)) for o, i in zip(early, at)]
    choice_masks, flag_at = [], {}
    for o, names in enumerate(choices):
        if o not in early:
            flag_at[o] = len(choice_masks)
            for i in range(len(names) - 1):
                choice_masks.append(sum(int(picks[r, o] == i) << r for r in range(chips)))
    flags_shape = jax.ShapeDtypeStruct((max(8, len(choice_masks)), SLOTS * TILE), jnp.float32)
    *sent, flags = pl.pallas_call(
        functools.partial(units_kernel, min(packed, default=chips), masks, choice_masks),
        out_shape=(unit_shape,) * (2 + len(early)) + (flags_shape,),
        in_specs=[HBM, HBM],
        out_specs=(VMEM,) * (3 + len(early)),
        scratch_shapes=[
            pltpu.SMEM(a_fill.shape, a_fill.dtype),
            pltpu.VMEM(a_band.shape, a_band.dtype),
            pltpu.SemaphoreType.DMA((2,)),
        ],
        compiler_params=params,
        name="units",
    )(fill, band)
    n0, n1, *sent = sent
    buffers = {"n0": n0, "n1": n1}
    payload = left = sums = None
    added = 0

    def start():
        return pl.pallas_call(
            functools.partial(first_kernel, 0),
            out_shape=(
                jax.ShapeDtypeStruct((NO_TERM + 1, 2 * TILE, TILE), jnp.bfloat16),
                token_shape,
                sums_shape,
            ),
            in_specs=[SMEM, SMEM, VMEM, VMEM, VMEM],
            out_specs=(VMEM, VMEM, VMEM),
            compiler_params=params,
            name="first",
        )(table, a_fill, a_band, n0, n1)

    def more(after, sums, units, base):
        return pl.pallas_call(
            functools.partial(more_kernel, base),
            out_shape=(token_shape, sums_shape),
            in_specs=[SMEM] + [VMEM] * (3 + len(units)),
            out_specs=(VMEM, VMEM),
            input_output_aliases={3 + len(units): 1},
            compiler_params=params,
            name="more",
        )(table, left, after, *units, sums)

    for o, moves in enumerate(ops):
        sources = [buffers[n] for n in choices[o]]
        if o in early:
            payload = sent[early.index(o)]
        else:
            order = 0 * payload[:1].astype(jnp.float32) if o > 0 else 0
            if o == FIRST:
                left, token, sums = start()
                order += token
            elif o in ADD_AT:
                units = [buffers[n] for n in range(added, o - LAG)]
                token, sums = more(payload, sums, units, 2 + added)
                added = o - LAG
                order += token
            payload = sources[-1]
            for i in reversed(range(len(sources) - 1)):
                at = flag_at[o] + i
                payload = jnp.where(flags[at : at + 1] + order > 0.5, sources[i], payload)
        buffers[o] = lax.ppermute(payload, RC, [(s, t) for s, t, _ in moves])
    if sums is None:
        left, _, sums = start()
    for count in LAST:
        units = [buffers[n] for n in range(added, len(ops) - count)]
        _, sums = more(units[0], sums, units, 2 + added)
        added += len(units)

    piece = jax.ShapeDtypeStruct((2, OUT_BAND // 2, TILE // 2, TILE), jnp.bfloat16)
    units = [buffers[n] for n in range(added, len(ops))]
    n_in = 3 + len(units)
    kept, given, _ = pl.pallas_call(
        functools.partial(last_kernel, 2 + added),
        out_shape=(piece, piece, sums_shape),
        in_specs=[SMEM, SMEM] + [VMEM] * (n_in - 1),
        out_specs=(VMEM, VMEM, VMEM),
        input_output_aliases={n_in: 2},
        compiler_params=params,
        name="last",
    )(table, c_reach, left, *units, sums)
    taken = lax.ppermute(given, "depth", [(0, 1), (1, 0)])
    return pl.pallas_call(
        join_kernel,
        out_shape=jax.ShapeDtypeStruct((2, OUT_BAND, TILE // 2, TILE), jnp.bfloat16),
        in_specs=[VMEM, VMEM],
        out_specs=VMEM,
        compiler_params=params,
        name="join",
    )(kept, taken)


def solution(mesh):
    rows, cols = mesh.shape["row"], mesh.shape["col"]
    plan = grid_plan() if (rows, cols) == (4, 4) else direct_plan(rows * cols)
    in_specs = (P(RC, None, None, None), P(RC, None), P(RC))
    out_specs = P(RC, None, "depth", None)
    return jax.shard_map(
        functools.partial(per_device, plan, rows * cols),
        mesh=mesh,
        in_specs=in_specs,
        out_specs=out_specs,
        check_vma=False,
    )
```

```python
import functools

import jax
import jax.numpy as jnp
import numpy as np
from jax import lax
from jax.experimental import pallas as pl
from jax.experimental.pallas import tpu as pltpu
from jax.sharding import PartitionSpec as P

OUT_BAND = 24
TILE = 128
SLOTS = 8
SUMS = 17
NO_TERM = 17
RC = ("row", "col")


STEPS = (
    (1, (
        (1, 1, 0), (3, 3, 1), (4, 4, 1), (5, 5, 1), (6, 6, 1), (7, 7, 1), (8, 8, 0), (9, 9, 0),
        (10, 10, 1), (11, 11, 1), (13, 13, 0), (14, 14, 0), (15, 15, 0),
    )),
    (0, (
        (2, 2, 0), (4, 4, 0), (5, 5, 0), (6, 6, 0), (7, 7, 1), (8, 8, 1), (9, 9, 0),
        (10, 10, 1), (11, 11, 1), (12, 12, 0), (14, 14, 0), (15, 15, 0),
    )),
    (8, (
        (2, 2, 1), (4, 4, 1), (5, 5, 1), (6, 6, 1), (8, 8, 0), (9, 9, 1), (10, 10, 0),
        (11, 11, 0), (12, 12, 0), (13, 13, 0), (14, 14, 0), (15, 15, 0),
    )),
    (1, (
        (1, 1, 1), (3, 3, 0), (4, 4, 0), (5, 5, 0), (6, 6, 0), (7, 7, 0), (8, 8, 1), (9, 9, 1),
        (10, 10, 0), (11, 11, 0),
    )),
    (0, (
        (2, 3, 1), (4, 5, 1), (5, 4, 1), (6, 6, 1), (7, 6, 1), (8, 9, 0), (10, 10, 0),
        (12, 13, 0), (14, 15, 0), (15, 14, 0),
    )),
    (9, (
        (1, 5, 0), (2, 6, 0), (5, 4, 1), (6, 7, 1), (8, 9, 0), (9, 8, 0), (10, 11, 1),
        (11, 10, 1), (12, 8, 1), (13, 9, 0), (14, 10, 1), (15, 14, 0),
    )),
    (1, (
        (0, 8, 0), (1, 5, 0), (3, 11, 0), (4, 12, 0), (5, 6, 1), (8, 12, 0), (13, 14, 0),
        (14, 13, 0),
    )),
    (0, (
        (0, 8, 0), (1, 9, 1), (2, 10, 0), (3, 11, 0), (4, 4, 1), (5, 6, 1), (6, 7, 1),
        (7, 7, 0), (11, 10, 0), (12, 4, 1), (13, 13, 0), (14, 13, 0),
    )),
    (9, (
        (1, 9, 1), (2, 3, 0), (4, 5, 0), (5, 4, 0), (6, 7, 0), (8, 9, 1), (9, 8, 1),
        (10, 2, 1), (11, 10, 0), (12, 9, 0), (14, 10, 0), (15, 11, 1),
    )),
    (1, (
        (0, 9, 0), (1, 6, 0), (2, 5, 0), (3, 10, 1), (4, 8, 1), (5, 7, 1), (6, 5, 1),
        (7, 14, 0), (9, 11, 1), (10, 8, 0), (13, 10, 1), (14, 9, 0),
    )),
    (0, (
        (1, 6, 0), (2, 11, 0), (3, 10, 1), (4, 6, 1), (5, 7, 1), (6, 5, 1), (7, 6, 0),
        (12, 14, 0), (14, 9, 0),
    )),
    (9, (
        (1, 4, 1), (2, 3, 1), (5, 12, 0), (6, 10, 0), (10, 11, 0), (12, 13, 0), (14, 15, 0),
        (15, 13, 0),
    )),
    (1, (
        (0, 4, 0), (1, 3, 0), (2, 9, 1), (3, 7, 0), (4, 9, 0), (5, 7, 0), (6, 4, 0),
        (7, 11, 1), (9, 2, 1), (10, 8, 1), (13, 10, 0),
    )),
    (0, (
        (0, 6, 0), (1, 8, 0), (2, 10, 1), (3, 10, 0), (4, 7, 1), (5, 8, 1), (7, 5, 1),
        (8, 11, 1), (9, 11, 1), (10, 8, 0), (11, 8, 0), (12, 10, 1), (13, 10, 1),
    )),
    (9, (
        (1, 9, 0), (2, 2, 0), (5, 8, 1), (6, 11, 0), (9, 12, 0), (10, 15, 0), (11, 8, 0),
        (12, 10, 1), (15, 9, 0),
    )),
    (1, (
        (0, 5, 1), (1, 3, 1), (2, 4, 1), (4, 13, 0), (5, 10, 0), (6, 12, 0), (7, 13, 0),
        (8, 14, 0), (9, 11, 0), (10, 13, 0), (13, 15, 0),
    )),
    (0, (
        (0, 9, 1), (2, 9, 1), (3, 9, 1), (4, 7, 0), (5, 7, 0), (6, 4, 0), (7, 4, 0),
        (12, 10, 0), (13, 10, 0),
    )),
    (7, (
        (1, 8, 1), (2, 2, 1), (8, 2, 1), (11, 8, 1), (12, 11, 1), (13, 11, 1), (14, 8, 0),
        (15, 8, 0),
    )),
    (1, (
        (1, 2, 0), (2, 9, 0), (3, 8, 0), (4, 10, 1), (5, 11, 0), (6, 8, 1), (7, 9, 0),
        (9, 15, 0), (10, 12, 0),
    )),
)


def partner(kind, chip):
    z, row = chip % 4, chip // 4
    if kind < 6:
        return chip ^ (4, 1, 8, 2, 3, 12)[kind]
    if z in (1, 2) and (kind - 6) >> (row % 2) & 1:
        return chip ^ 3
    return chip ^ 8


def grid_plan():
    ops = []
    for kind, sends in STEPS:
        sent = {source: (block, part) for source, block, part in sends}
        ops.append([(c, partner(kind, c), sent.get(c)) for c in range(16)])
    return ops, frozenset(range(12, 16))


def direct_plan(chips):
    ops = []
    for m in range(1, 9):
        for part in range(2 if m < 8 else 1):
            ops.append([(r + m, r, (r + m, part)) for r in range(chips - m)])
    return ops, frozenset()


def first_slot(k, core):
    return (k - core + ((core + k) & 1)) // 2


def left_tiles(block, part, chip, packed):
    m = block - chip
    ks = [2 * m + part] * 2
    if packed:
        ks = [2 * m, 2 * m + 1] if part == 0 else [NO_TERM, NO_TERM]
    return [k if m >= 0 and k < NO_TERM else NO_TERM for k in ks]


def by_chip(values, chip):
    if len(set(values)) == 1:
        return values[0]
    word = 0
    for at in range(0, len(values), 6):
        bits = sum(v << 5 * i for i, v in enumerate(values[at : at + 6]))
        word = jnp.where(chip >= at, bits, word)
    return (word >> 5 * (chip % 6)) & 31


def position():
    chip = lax.axis_index("row") * lax.axis_size("col") + lax.axis_index("col")
    return chip, lax.axis_index("depth")


VMEM = pl.BlockSpec(memory_space=pltpu.VMEM)
SMEM = pl.BlockSpec(memory_space=pltpu.SMEM)
HBM = pl.BlockSpec(memory_space=pltpu.HBM)
VMEM_LIMIT = 12 * 2**20
FIRST = 4
LAG = 4
ADD_AT = (9, 12, 15, 18)
LAST = (2, 1)


def units_kernel(packed_from, choice_masks, fill_hbm, band_hbm, *refs):
    outs, flags, (fill_ref, band_ref, sems) = refs[:2], refs[2], refs[3:]
    fill_copy = pltpu.make_async_copy(fill_hbm, fill_ref, sems.at[2])
    copies = [
        pltpu.make_async_copy(band_hbm.at[row], band_ref.at[row], sems.at[row]) for row in range(2)
    ]
    for copy in (fill_copy, *copies):
        copy.start()
    chip, core = position()
    for i, mask in enumerate(choice_masks):
        bit = ((mask >> chip) & 1).astype(jnp.float32)
        flags[i : i + 1, :] = jnp.full((1, flags.shape[1]), bit, flags.dtype)
    packed = chip >= packed_from
    for copy in (fill_copy, *copies):
        copy.wait()
    for part, unit in enumerate(outs):
        for slot in range(SLOTS):
            row, t = part, slot
            if part == 0:
                row = jnp.where(packed, slot // 4, 0)
                t = jnp.where(packed, slot % 4, slot)
            entry = 2 * t + ((core + row) & 1)
            fill = fill_ref[row, entry].astype(jnp.float32)
            tile = band_ref[row, entry].astype(jnp.float32) * fill
            unit[:, slot * TILE : (slot + 1) * TILE] = tile.astype(jnp.bfloat16)


def add_terms(terms, left_ref, units, sums):
    width = SLOTS // 2 * TILE
    chip, core = position()
    for (first, second), unit in zip(terms, units):
        ks = [by_chip(first, chip), by_chip(second, chip)]
        slots = [first_slot(k, core) for k in ks]
        slots[1] = jnp.where(ks[0] == ks[1], slots[0] + SLOTS // 2, slots[1])
        for half, (k, slot) in enumerate(zip(ks, slots)):
            product = jnp.dot(
                left_ref[k],
                unit[:, half * width : (half + 1) * width],
                preferred_element_type=jnp.float32,
            )
            for q in range(SLOTS // 2):
                sums[slot + q] += product[:, q * TILE : (q + 1) * TILE]


def first_kernel(terms, reach_hbm, fill_hbm, band_hbm, *refs):
    units, (left, keep, token, sums) = refs[:2], refs[2:6]
    reach_ref, fill_ref, band_ref, sems = refs[6:]
    copies = [
        pltpu.make_async_copy(source, target, sems.at[i])
        for i, (source, target) in enumerate(
            [(reach_hbm, reach_ref), (fill_hbm, fill_ref), (band_hbm, band_ref)]
        )
    ]
    for copy in copies:
        copy.start()
    sums[...] = jnp.zeros(sums.shape, jnp.float32)
    for copy in copies:
        copy.wait()
    token[...] = jnp.zeros(token.shape, token.dtype)
    _, core = position()
    for row in range(2):
        for s in range(OUT_BAND // 2):
            kept = 2 * s + ((core + row) & 1) < reach_ref[row]
            value = jnp.where(kept, 1.0, 0.0).astype(jnp.float32)
            keep[row, s : s + 1, :] = jnp.full((1, TILE), value, jnp.float32)
    zero = jnp.zeros((TILE, TILE), jnp.bfloat16)
    left[0, TILE:] = zero
    left[16, :TILE] = zero
    left[NO_TERM] = jnp.zeros((2 * TILE, TILE), jnp.bfloat16)
    for row in range(2):
        for entry in range(16):
            fill = fill_ref[row, entry].astype(jnp.float32)
            tile = band_ref[row, entry].astype(jnp.float32) * fill
            left[entry + row, row * TILE : (row + 1) * TILE] = tile.astype(jnp.bfloat16)
    add_terms(terms, left, units, sums)


def more_kernel(terms, left_ref, after_ref, *refs):
    units, (token, sums) = refs[:-3], refs[-2:]
    token[...] = jnp.zeros(token.shape, token.dtype)
    add_terms(terms, left_ref, units, sums)


def last_kernel(terms, left_ref, keep_ref, *refs):
    units, kept, given, sums = refs[:-4], refs[-3], refs[-2], refs[-1]
    add_terms(terms, left_ref, units, sums)
    _, core = position()
    half = TILE // 2
    for row in range(2):
        shift = 0 if row == 0 else 1 - core
        for s in range(OUT_BAND // 2):
            keep = keep_ref[row, s : s + 1, :] > 0.5
            for out, side in ((kept, core), (given, 1 - core)):
                start = pl.multiple_of(row * TILE + side * half, half)
                tile = sums[s + shift, pl.ds(start, half), :]
                out[row, s] = jnp.where(keep, tile, 0.0).astype(jnp.bfloat16)


def place_kernel(partner, tiles, *refs):
    out, sems = refs[-2:]
    _, core = position()
    copies = []
    for row in range(2):
        odd = (core + row + partner) & 1
        copies.append(pltpu.make_async_copy(tiles.at[row], out.at[row, :, odd], sems.at[row]))
    for copy in copies:
        copy.start()
    for copy in copies:
        copy.wait()


def lookup(plan, chips):
    ops, packed = plan
    held = {"n0": [(r, 0) for r in range(chips)], "n1": [(r, 1) for r in range(chips)]}
    order = ["n0", "n1"] + list(range(len(ops)))
    picks = np.zeros((chips, len(ops)), np.int32)
    choices = []
    for o, moves in enumerate(ops):
        names = []
        got = [None] * chips
        for source, target, unit in moves:
            if unit is None:
                continue
            name = next(n for n in order if n in held and held[n][source] == unit)
            if name not in names:
                names.append(name)
            picks[source, o] = names.index(name)
            got[target] = unit
        held[o] = got
        choices.append(names)
    terms = {n: [[], []] for n in order}
    for r in range(chips):
        done = set()
        for n in order:
            unit = held[n][r]
            fresh = unit is not None and unit not in done
            done.add(unit)
            ks = left_tiles(*unit, r, unit[0] in packed) if fresh else [NO_TERM] * 2
            for half in range(2):
                terms[n][half].append(ks[half])
    if not packed:
        terms = {n: [[max(k, key=k.count)] for k in ks] for n, ks in terms.items()}
    return terms, picks, choices


def per_device(plan, chips, a_band, a_fill, c_reach):
    ops, packed = plan
    terms, picks, choices = lookup(plan, chips)
    reach = pltpu.with_memory_space_constraint(c_reach, pltpu.HBM)
    fill = pltpu.with_memory_space_constraint(a_fill, pltpu.HBM)
    band = pltpu.with_memory_space_constraint(a_band, pltpu.HBM)
    params = pltpu.CompilerParams(vmem_limit_bytes=VMEM_LIMIT)
    unit_shape = jax.ShapeDtypeStruct((TILE, SLOTS * TILE), jnp.bfloat16)
    token_shape = jax.ShapeDtypeStruct((1, SLOTS * TILE), jnp.float32)
    sums_shape = jax.ShapeDtypeStruct((SUMS, 2 * TILE, TILE), jnp.float32)
    choice_masks, flag_at = [], {}
    for o, names in enumerate(choices):
        flag_at[o] = len(choice_masks)
        for i in range(len(names) - 1):
            choice_masks.append(sum(int(picks[r, o] == i) << r for r in range(chips)))
    flags_shape = jax.ShapeDtypeStruct((max(8, len(choice_masks)), SLOTS * TILE), jnp.float32)
    n0, n1, flags = pl.pallas_call(
        functools.partial(units_kernel, min(packed, default=chips), choice_masks),
        out_shape=(unit_shape, unit_shape, flags_shape),
        in_specs=[HBM, HBM],
        out_specs=(VMEM,) * 3,
        scratch_shapes=[
            pltpu.SMEM(a_fill.shape, a_fill.dtype),
            pltpu.VMEM(a_band.shape, a_band.dtype),
            pltpu.SemaphoreType.DMA((3,)),
        ],
        compiler_params=params,
        name="units",
    )(fill, band)
    buffers = {"n0": n0, "n1": n1}
    payload = left = keep = sums = None
    added = 0

    def start():
        return pl.pallas_call(
            functools.partial(first_kernel, [terms["n0"], terms["n1"]]),
            out_shape=(
                jax.ShapeDtypeStruct((NO_TERM + 1, 2 * TILE, TILE), jnp.bfloat16),
                jax.ShapeDtypeStruct((2, OUT_BAND // 2, TILE), jnp.float32),
                token_shape,
                sums_shape,
            ),
            in_specs=[HBM, HBM, HBM, VMEM, VMEM],
            out_specs=(VMEM,) * 4,
            scratch_shapes=[
                pltpu.SMEM(c_reach.shape, c_reach.dtype),
                pltpu.SMEM(a_fill.shape, a_fill.dtype),
                pltpu.VMEM(a_band.shape, a_band.dtype),
                pltpu.SemaphoreType.DMA((3,)),
            ],
            compiler_params=params,
            name="first",
        )(reach, fill, band, n0, n1)

    def more(after, sums, names):
        units = [buffers[n] for n in names]
        return pl.pallas_call(
            functools.partial(more_kernel, [terms[n] for n in names]),
            out_shape=(token_shape, sums_shape),
            in_specs=[VMEM] * (3 + len(units)),
            out_specs=(VMEM, VMEM),
            input_output_aliases={2 + len(units): 1},
            compiler_params=params,
            name="more",
        )(left, after, *units, sums)

    for o, moves in enumerate(ops):
        sources = [buffers[n] for n in choices[o]]
        order = 0 * payload[:1].astype(jnp.float32) if o > 0 else 0
        if o == FIRST:
            left, keep, token, sums = start()
            order += token
        elif o in ADD_AT:
            token, sums = more(payload, sums, range(added, o - LAG))
            added = o - LAG
            order += token
        payload = sources[-1]
        if len(sources) == 1:
            payload = jnp.where(order > 0.5, n0, payload)
        for i in reversed(range(len(sources) - 1)):
            at = flag_at[o] + i
            payload = jnp.where(flags[at : at + 1] + order > 0.5, sources[i], payload)
        buffers[o] = lax.ppermute(payload, RC, [(s, t) for s, t, _ in moves])
    if sums is None:
        left, keep, _, sums = start()
    for count in LAST:
        _, sums = more(buffers[added], sums, range(added, len(ops) - count))
        added = len(ops) - count

    piece = jax.ShapeDtypeStruct((2, OUT_BAND // 2, TILE // 2, TILE), jnp.bfloat16)
    units = [buffers[n] for n in range(added, len(ops))]
    n_in = 2 + len(units)
    kept, given, _ = pl.pallas_call(
        functools.partial(last_kernel, [terms[n] for n in range(added, len(ops))]),
        out_shape=(piece, piece, sums_shape),
        in_specs=[VMEM] * (n_in + 1),
        out_specs=(VMEM, VMEM, VMEM),
        input_output_aliases={n_in: 2},
        compiler_params=params,
        name="last",
    )(left, keep, *units, sums)
    taken = lax.ppermute(given, "depth", [(0, 1), (1, 0)])
    out = None
    for partner, tiles in enumerate((kept, taken)):
        out = pl.pallas_call(
            functools.partial(place_kernel, partner),
            out_shape=jax.ShapeDtypeStruct(
                (2, OUT_BAND // 2, 2, TILE // 2, TILE), jnp.bfloat16
            ),
            in_specs=[VMEM, HBM][: 1 + partner],
            out_specs=HBM,
            scratch_shapes=[pltpu.SemaphoreType.DMA((2,))],
            input_output_aliases={1: 0} if partner else {},
            compiler_params=params,
            name="place",
        )(*[tiles, out][: 1 + partner])
    return out.reshape(2, OUT_BAND, TILE // 2, TILE)


def solution(mesh):
    rows, cols = mesh.shape["row"], mesh.shape["col"]
    plan = grid_plan() if (rows, cols) == (4, 4) else direct_plan(rows * cols)
    in_specs = (P(RC, None, None, None), P(RC, None), P(RC))
    out_specs = P(RC, None, "depth", None)
    return jax.shard_map(
        functools.partial(per_device, plan, rows * cols),
        mesh=mesh,
        in_specs=in_specs,
        out_specs=out_specs,
        check_vma=False,
    )
```

```python
import functools

import jax
import jax.numpy as jnp
import numpy as np
from jax import lax
from jax.experimental import pallas as pl
from jax.experimental.pallas import tpu as pltpu
from jax.sharding import PartitionSpec as P

OUT_BAND = 24
TILE = 128
SLOTS = 8
SUMS = 17
NO_TERM = 17
RC = ("row", "col")


STEPS = (
    (1, (
        (1, 1, 0), (3, 3, 1), (4, 4, 1), (5, 5, 1), (6, 6, 1), (7, 7, 1), (8, 8, 0), (9, 9, 0),
        (10, 10, 1), (11, 11, 1), (13, 13, 0), (14, 14, 0), (15, 15, 0),
    )),
    (0, (
        (2, 2, 0), (4, 4, 0), (5, 5, 0), (6, 6, 0), (7, 7, 1), (8, 8, 1), (9, 9, 0),
        (10, 10, 1), (11, 11, 1), (12, 12, 0), (14, 14, 0), (15, 15, 0),
    )),
    (8, (
        (2, 2, 1), (4, 4, 1), (5, 5, 1), (6, 6, 1), (8, 8, 0), (9, 9, 1), (10, 10, 0),
        (11, 11, 0), (12, 12, 0), (13, 13, 0), (14, 14, 0), (15, 15, 0),
    )),
    (1, (
        (1, 1, 1), (3, 3, 0), (4, 4, 0), (5, 5, 0), (6, 6, 0), (7, 7, 0), (8, 8, 1), (9, 9, 1),
        (10, 10, 0), (11, 11, 0),
    )),
    (0, (
        (2, 3, 1), (4, 5, 1), (5, 4, 1), (6, 6, 1), (7, 6, 1), (8, 9, 0), (10, 10, 0),
        (12, 13, 0), (14, 15, 0), (15, 14, 0),
    )),
    (9, (
        (1, 5, 0), (2, 6, 0), (5, 4, 1), (6, 7, 1), (8, 9, 0), (9, 8, 0), (10, 11, 1),
        (11, 10, 1), (12, 8, 1), (13, 9, 0), (14, 10, 1), (15, 14, 0),
    )),
    (1, (
        (0, 8, 0), (1, 5, 0), (3, 11, 0), (4, 12, 0), (5, 6, 1), (8, 12, 0), (13, 14, 0),
        (14, 13, 0),
    )),
    (0, (
        (0, 8, 0), (1, 9, 1), (2, 10, 0), (3, 11, 0), (4, 4, 1), (5, 6, 1), (6, 7, 1),
        (7, 7, 0), (11, 10, 0), (12, 4, 1), (13, 13, 0), (14, 13, 0),
    )),
    (9, (
        (1, 9, 1), (2, 3, 0), (4, 5, 0), (5, 4, 0), (6, 7, 0), (8, 9, 1), (9, 8, 1),
        (10, 2, 1), (11, 10, 0), (12, 9, 0), (14, 10, 0), (15, 11, 1),
    )),
    (1, (
        (0, 9, 0), (1, 6, 0), (2, 5, 0), (3, 10, 1), (4, 8, 1), (5, 7, 1), (6, 5, 1),
        (7, 14, 0), (9, 11, 1), (10, 8, 0), (13, 10, 1), (14, 9, 0),
    )),
    (0, (
        (1, 6, 0), (2, 11, 0), (3, 10, 1), (4, 6, 1), (5, 7, 1), (6, 5, 1), (7, 6, 0),
        (12, 14, 0), (14, 9, 0),
    )),
    (9, (
        (1, 4, 1), (2, 3, 1), (5, 12, 0), (6, 10, 0), (10, 11, 0), (12, 13, 0), (14, 15, 0),
        (15, 13, 0),
    )),
    (1, (
        (0, 4, 0), (1, 3, 0), (2, 9, 1), (3, 7, 0), (4, 9, 0), (5, 7, 0), (6, 4, 0),
        (7, 11, 1), (9, 2, 1), (10, 8, 1), (13, 10, 0),
    )),
    (0, (
        (0, 6, 0), (1, 8, 0), (2, 10, 1), (3, 10, 0), (4, 7, 1), (5, 8, 1), (7, 5, 1),
        (8, 11, 1), (9, 11, 1), (10, 8, 0), (11, 8, 0), (12, 10, 1), (13, 10, 1),
    )),
    (9, (
        (1, 9, 0), (2, 2, 0), (5, 8, 1), (6, 11, 0), (9, 12, 0), (10, 15, 0), (11, 8, 0),
        (12, 10, 1), (15, 9, 0),
    )),
    (1, (
        (0, 5, 1), (1, 3, 1), (2, 4, 1), (4, 13, 0), (5, 10, 0), (6, 12, 0), (7, 13, 0),
        (8, 14, 0), (9, 11, 0), (10, 13, 0), (13, 15, 0),
    )),
    (0, (
        (0, 9, 1), (2, 9, 1), (3, 9, 1), (4, 7, 0), (5, 7, 0), (6, 4, 0), (7, 4, 0),
        (12, 10, 0), (13, 10, 0),
    )),
    (7, (
        (1, 8, 1), (2, 2, 1), (8, 2, 1), (11, 8, 1), (12, 11, 1), (13, 11, 1), (14, 8, 0),
        (15, 8, 0),
    )),
    (1, (
        (1, 2, 0), (2, 9, 0), (3, 8, 0), (4, 10, 1), (5, 11, 0), (6, 8, 1), (7, 9, 0),
        (9, 15, 0), (10, 12, 0),
    )),
)


def partner(kind, chip):
    z, row = chip % 4, chip // 4
    if kind < 6:
        return chip ^ (4, 1, 8, 2, 3, 12)[kind]
    if z in (1, 2) and (kind - 6) >> (row % 2) & 1:
        return chip ^ 3
    return chip ^ 8


def grid_plan():
    ops = []
    for kind, sends in STEPS:
        sent = {source: (block, part) for source, block, part in sends}
        ops.append([(c, partner(kind, c), sent.get(c)) for c in range(16)])
    return ops, frozenset(range(12, 16))


def direct_plan(chips):
    ops = []
    for m in range(1, 9):
        for part in range(2 if m < 8 else 1):
            ops.append([(r + m, r, (r + m, part)) for r in range(chips - m)])
    return ops, frozenset()


def first_slot(k, core):
    return (k - core + ((core + k) & 1)) // 2


def left_tiles(block, part, chip, packed):
    m = block - chip
    ks = [2 * m + part] * 2
    if packed:
        ks = [2 * m, 2 * m + 1] if part == 0 else [NO_TERM, NO_TERM]
    return [k if m >= 0 and k < NO_TERM else NO_TERM for k in ks]


def by_chip(values, chip):
    if len(set(values)) == 1:
        return values[0]
    word = 0
    for at in range(0, len(values), 6):
        bits = sum(v << 5 * i for i, v in enumerate(values[at : at + 6]))
        word = jnp.where(chip >= at, bits, word)
    return (word >> 5 * (chip % 6)) & 31


def position():
    chip = lax.axis_index("row") * lax.axis_size("col") + lax.axis_index("col")
    return chip, lax.axis_index("depth")


VMEM = pl.BlockSpec(memory_space=pltpu.VMEM)
SMEM = pl.BlockSpec(memory_space=pltpu.SMEM)
HBM = pl.BlockSpec(memory_space=pltpu.HBM)
VMEM_LIMIT = 12 * 2**20
FIRST = 4
LAG = 4
ADD_AT = (9, 12, 16)
LAST = (2, 1)


def units_kernel(packed_from, choice_masks, fill_hbm, band_hbm, *refs):
    outs, flags, (fill_ref, band_ref, sems) = refs[:2], refs[2], refs[3:]
    fill_copy = pltpu.make_async_copy(fill_hbm, fill_ref, sems.at[2])
    copies = [
        pltpu.make_async_copy(band_hbm.at[row], band_ref.at[row], sems.at[row]) for row in range(2)
    ]
    for copy in (fill_copy, *copies):
        copy.start()
    chip, core = position()
    for i, mask in enumerate(choice_masks):
        bit = ((mask >> chip) & 1).astype(jnp.float32)
        flags[i : i + 1, :] = jnp.full((1, flags.shape[1]), bit, flags.dtype)
    packed = chip >= packed_from
    for copy in (fill_copy, *copies):
        copy.wait()
    for part, unit in enumerate(outs):
        for slot in range(SLOTS):
            row, t = part, slot
            if part == 0:
                row = jnp.where(packed, slot // 4, 0)
                t = jnp.where(packed, slot % 4, slot)
            entry = 2 * t + ((core + row) & 1)
            fill = fill_ref[row, entry].astype(jnp.float32)
            tile = band_ref[row, entry].astype(jnp.float32) * fill
            unit[:, slot * TILE : (slot + 1) * TILE] = tile.astype(jnp.bfloat16)


def add_terms(terms, left_ref, units, sums):
    width = SLOTS // 2 * TILE
    chip, core = position()
    for (first, second), unit in zip(terms, units):
        ks = [by_chip(first, chip), by_chip(second, chip)]
        slots = [first_slot(k, core) for k in ks]
        slots[1] = jnp.where(ks[0] == ks[1], slots[0] + SLOTS // 2, slots[1])
        for half, (k, slot) in enumerate(zip(ks, slots)):
            product = jnp.dot(
                left_ref[k],
                unit[:, half * width : (half + 1) * width],
                preferred_element_type=jnp.float32,
            )
            for q in range(SLOTS // 2):
                sums[slot + q] += product[:, q * TILE : (q + 1) * TILE]


def first_kernel(terms, reach_hbm, fill_hbm, band_hbm, *refs):
    units, (left, keep, token, sums) = refs[:2], refs[2:6]
    reach_ref, fill_ref, band_ref, sems = refs[6:]
    copies = [
        pltpu.make_async_copy(source, target, sems.at[i])
        for i, (source, target) in enumerate(
            [(reach_hbm, reach_ref), (fill_hbm, fill_ref), (band_hbm, band_ref)]
        )
    ]
    for copy in copies:
        copy.start()
    sums[...] = jnp.zeros(sums.shape, jnp.float32)
    for copy in copies:
        copy.wait()
    token[...] = jnp.zeros(token.shape, token.dtype)
    _, core = position()
    for row in range(2):
        for s in range(OUT_BAND // 2):
            kept = 2 * s + ((core + row) & 1) < reach_ref[row]
            value = jnp.where(kept, 1.0, 0.0).astype(jnp.float32)
            keep[row, s : s + 1, :] = jnp.full((1, TILE), value, jnp.float32)
    zero = jnp.zeros((TILE, TILE), jnp.bfloat16)
    left[0, TILE:] = zero
    left[16, :TILE] = zero
    left[NO_TERM] = jnp.zeros((2 * TILE, TILE), jnp.bfloat16)
    for row in range(2):
        for entry in range(16):
            fill = fill_ref[row, entry].astype(jnp.float32)
            tile = band_ref[row, entry].astype(jnp.float32) * fill
            left[entry + row, row * TILE : (row + 1) * TILE] = tile.astype(jnp.bfloat16)
    add_terms(terms, left, units, sums)


def more_kernel(terms, left_ref, after_ref, *refs):
    units, sums = refs[: len(terms)], refs[-1]
    for token in refs[len(terms) + 1 : -1]:
        token[...] = jnp.zeros(token.shape, token.dtype)
    add_terms(terms, left_ref, units, sums)


def last_kernel(terms, left_ref, keep_ref, *refs):
    units, kept, given, sums = refs[:-4], refs[-3], refs[-2], refs[-1]
    add_terms(terms, left_ref, units, sums)
    _, core = position()
    half = TILE // 2
    for row in range(2):
        shift = 0 if row == 0 else 1 - core
        for s in range(OUT_BAND // 2):
            keep = keep_ref[row, s : s + 1, :] > 0.5
            for out, side in ((kept, core), (given, 1 - core)):
                start = pl.multiple_of(row * TILE + side * half, half)
                tile = sums[s + shift, pl.ds(start, half), :]
                out[row, s] = jnp.where(keep, tile, 0.0).astype(jnp.bfloat16)


def place_kernel(partner, tiles, *refs):
    out, sems = refs[-2:]
    _, core = position()
    copies = []
    for row in range(2):
        odd = (core + row + partner) & 1
        copies.append(pltpu.make_async_copy(tiles.at[row], out.at[row, :, odd], sems.at[row]))
    for copy in copies:
        copy.start()
    for copy in copies:
        copy.wait()


def lookup(plan, chips):
    ops, packed = plan
    held = {"n0": [(r, 0) for r in range(chips)], "n1": [(r, 1) for r in range(chips)]}
    order = ["n0", "n1"] + list(range(len(ops)))
    picks = np.zeros((chips, len(ops)), np.int32)
    choices = []
    for o, moves in enumerate(ops):
        names = []
        got = [None] * chips
        for source, target, unit in moves:
            if unit is None:
                continue
            name = next(n for n in order if n in held and held[n][source] == unit)
            if name not in names:
                names.append(name)
            picks[source, o] = names.index(name)
            got[target] = unit
        held[o] = got
        choices.append(names)
    terms = {n: [[], []] for n in order}
    for r in range(chips):
        done = set()
        for n in order:
            unit = held[n][r]
            fresh = unit is not None and unit not in done
            done.add(unit)
            ks = left_tiles(*unit, r, unit[0] in packed) if fresh else [NO_TERM] * 2
            for half in range(2):
                terms[n][half].append(ks[half])
    if not packed:
        terms = {n: [[max(k, key=k.count)] for k in ks] for n, ks in terms.items()}
    return terms, picks, choices


def per_device(plan, chips, a_band, a_fill, c_reach):
    ops, packed = plan
    terms, picks, choices = lookup(plan, chips)
    reach = pltpu.with_memory_space_constraint(c_reach, pltpu.HBM)
    fill = pltpu.with_memory_space_constraint(a_fill, pltpu.HBM)
    band = pltpu.with_memory_space_constraint(a_band, pltpu.HBM)
    params = pltpu.CompilerParams(vmem_limit_bytes=VMEM_LIMIT)
    unit_shape = jax.ShapeDtypeStruct((TILE, SLOTS * TILE), jnp.bfloat16)
    token_shape = jax.ShapeDtypeStruct((1, SLOTS * TILE), jnp.float32)
    sums_shape = jax.ShapeDtypeStruct((SUMS, 2 * TILE, TILE), jnp.float32)
    choice_masks, flag_at = [], {}
    for o, names in enumerate(choices):
        flag_at[o] = len(choice_masks)
        for i in range(len(names) - 1):
            choice_masks.append(sum(int(picks[r, o] == i) << r for r in range(chips)))
    flags_shape = jax.ShapeDtypeStruct((max(8, len(choice_masks)), SLOTS * TILE), jnp.float32)
    n0, n1, flags = pl.pallas_call(
        functools.partial(units_kernel, min(packed, default=chips), choice_masks),
        out_shape=(unit_shape, unit_shape, flags_shape),
        in_specs=[HBM, HBM],
        out_specs=(VMEM,) * 3,
        scratch_shapes=[
            pltpu.SMEM(a_fill.shape, a_fill.dtype),
            pltpu.VMEM(a_band.shape, a_band.dtype),
            pltpu.SemaphoreType.DMA((3,)),
        ],
        compiler_params=params,
        name="units",
    )(fill, band)
    buffers = {"n0": n0, "n1": n1}
    payload = left = keep = sums = None
    added = 0

    def start():
        return pl.pallas_call(
            functools.partial(first_kernel, [terms["n0"], terms["n1"]]),
            out_shape=(
                jax.ShapeDtypeStruct((NO_TERM + 1, 2 * TILE, TILE), jnp.bfloat16),
                jax.ShapeDtypeStruct((2, OUT_BAND // 2, TILE), jnp.float32),
                token_shape,
                sums_shape,
            ),
            in_specs=[HBM, HBM, HBM, VMEM, VMEM],
            out_specs=(VMEM,) * 4,
            scratch_shapes=[
                pltpu.SMEM(c_reach.shape, c_reach.dtype),
                pltpu.SMEM(a_fill.shape, a_fill.dtype),
                pltpu.VMEM(a_band.shape, a_band.dtype),
                pltpu.SemaphoreType.DMA((3,)),
            ],
            compiler_params=params,
            name="first",
        )(reach, fill, band, n0, n1)

    def more(after, sums, names, tokens=1):
        units = [buffers[n] for n in names]
        return pl.pallas_call(
            functools.partial(more_kernel, [terms[n] for n in names]),
            out_shape=(token_shape,) * tokens + (sums_shape,),
            in_specs=[VMEM] * (3 + len(units)),
            out_specs=(VMEM,) * (tokens + 1),
            input_output_aliases={2 + len(units): tokens},
            compiler_params=params,
            name="more",
        )(left, after, *units, sums)

    for o, moves in enumerate(ops):
        sources = [buffers[n] for n in choices[o]]
        order = 0 * payload[:1].astype(jnp.float32) if o > 0 else 0
        if o == FIRST:
            left, keep, token, sums = start()
            order += token
        elif o in ADD_AT:
            token, sums = more(payload, sums, range(added, o - LAG))
            added = o - LAG
            order += token
        payload = sources[-1]
        if len(sources) == 1:
            payload = jnp.where(order > 0.5, n0, payload)
        for i in reversed(range(len(sources) - 1)):
            at = flag_at[o] + i
            payload = jnp.where(flags[at : at + 1] + order > 0.5, sources[i], payload)
        buffers[o] = lax.ppermute(payload, RC, [(s, t) for s, t, _ in moves])
    if sums is None:
        left, keep, _, sums = start()
    for count in LAST:
        (sums,) = more(buffers[added], sums, range(added, len(ops) - count), tokens=0)
        added = len(ops) - count

    piece = jax.ShapeDtypeStruct((2, OUT_BAND // 2, TILE // 2, TILE), jnp.bfloat16)
    units = [buffers[n] for n in range(added, len(ops))]
    n_in = 2 + len(units)
    kept, given, _ = pl.pallas_call(
        functools.partial(last_kernel, [terms[n] for n in range(added, len(ops))]),
        out_shape=(piece, piece, sums_shape),
        in_specs=[VMEM] * (n_in + 1),
        out_specs=(VMEM, VMEM, VMEM),
        input_output_aliases={n_in: 2},
        compiler_params=params,
        name="last",
    )(left, keep, *units, sums)
    taken = lax.ppermute(given, "depth", [(0, 1), (1, 0)])
    out = None
    for partner, tiles in enumerate((kept, taken)):
        out = pl.pallas_call(
            functools.partial(place_kernel, partner),
            out_shape=jax.ShapeDtypeStruct(
                (2, OUT_BAND // 2, 2, TILE // 2, TILE), jnp.bfloat16
            ),
            in_specs=[VMEM, HBM][: 1 + partner],
            out_specs=HBM,
            scratch_shapes=[pltpu.SemaphoreType.DMA((2,))],
            input_output_aliases={1: 0} if partner else {},
            compiler_params=params,
            name="place",
        )(*[tiles, out][: 1 + partner])
    return out.reshape(2, OUT_BAND, TILE // 2, TILE)


def solution(mesh):
    rows, cols = mesh.shape["row"], mesh.shape["col"]
    plan = grid_plan() if (rows, cols) == (4, 4) else direct_plan(rows * cols)
    in_specs = (P(RC, None, None, None), P(RC, None), P(RC))
    out_specs = P(RC, None, "depth", None)
    return jax.shard_map(
        functools.partial(per_device, plan, rows * cols),
        mesh=mesh,
        in_specs=in_specs,
        out_specs=out_specs,
        check_vma=False,
    )
```

```python
import functools

import jax
import jax.numpy as jnp
import numpy as np
from jax import lax
from jax.experimental import pallas as pl
from jax.experimental.pallas import tpu as pltpu
from jax.sharding import PartitionSpec as P

OUT_BAND = 24
TILE = 128
SLOTS = 8
SUMS = 17
NO_TERM = 17
RC = ("row", "col")


STEPS = (
    (1, (
        (1, 1, 0), (3, 3, 1), (4, 4, 1), (5, 5, 1), (6, 6, 1), (7, 7, 1), (8, 8, 0), (9, 9, 0),
        (10, 10, 1), (11, 11, 1), (13, 13, 0), (14, 14, 0), (15, 15, 0),
    )),
    (0, (
        (2, 2, 0), (4, 4, 0), (5, 5, 0), (6, 6, 0), (7, 7, 1), (8, 8, 1), (9, 9, 0),
        (10, 10, 1), (11, 11, 1), (12, 12, 0), (14, 14, 0), (15, 15, 0),
    )),
    (8, (
        (2, 2, 1), (4, 4, 1), (5, 5, 1), (6, 6, 1), (8, 8, 0), (9, 9, 1), (10, 10, 0),
        (11, 11, 0), (12, 12, 0), (13, 13, 0), (14, 14, 0), (15, 15, 0),
    )),
    (1, (
        (1, 1, 1), (3, 3, 0), (4, 4, 0), (5, 5, 0), (6, 6, 0), (7, 7, 0), (8, 8, 1), (9, 9, 1),
        (10, 10, 0), (11, 11, 0),
    )),
    (0, (
        (2, 3, 1), (4, 5, 1), (5, 4, 1), (6, 6, 1), (7, 6, 1), (8, 9, 0), (10, 10, 0),
        (12, 13, 0), (14, 15, 0), (15, 14, 0),
    )),
    (9, (
        (1, 5, 0), (2, 6, 0), (5, 4, 1), (6, 7, 1), (8, 9, 0), (9, 8, 0), (10, 11, 1),
        (11, 10, 1), (12, 8, 1), (13, 9, 0), (14, 10, 1), (15, 14, 0),
    )),
    (1, (
        (0, 8, 0), (1, 5, 0), (3, 11, 0), (4, 12, 0), (5, 6, 1), (8, 12, 0), (13, 14, 0),
        (14, 13, 0),
    )),
    (0, (
        (0, 8, 0), (1, 9, 1), (2, 10, 0), (3, 11, 0), (4, 4, 1), (5, 6, 1), (6, 7, 1),
        (7, 7, 0), (11, 10, 0), (12, 4, 1), (13, 13, 0), (14, 13, 0),
    )),
    (9, (
        (1, 9, 1), (2, 3, 0), (4, 5, 0), (5, 4, 0), (6, 7, 0), (8, 9, 1), (9, 8, 1),
        (10, 2, 1), (11, 10, 0), (12, 9, 0), (14, 10, 0), (15, 11, 1),
    )),
    (1, (
        (0, 9, 0), (1, 6, 0), (2, 5, 0), (3, 10, 1), (4, 8, 1), (5, 7, 1), (6, 5, 1),
        (7, 14, 0), (9, 11, 1), (10, 8, 0), (13, 10, 1), (14, 9, 0),
    )),
    (0, (
        (1, 6, 0), (2, 11, 0), (3, 10, 1), (4, 6, 1), (5, 7, 1), (6, 5, 1), (7, 6, 0),
        (12, 14, 0), (14, 9, 0),
    )),
    (9, (
        (1, 4, 1), (2, 3, 1), (5, 12, 0), (6, 10, 0), (10, 11, 0), (12, 13, 0), (14, 15, 0),
        (15, 13, 0),
    )),
    (1, (
        (0, 4, 0), (1, 3, 0), (2, 9, 1), (3, 7, 0), (4, 9, 0), (5, 7, 0), (6, 4, 0),
        (7, 11, 1), (9, 2, 1), (10, 8, 1), (13, 10, 0),
    )),
    (0, (
        (0, 6, 0), (1, 8, 0), (2, 10, 1), (3, 10, 0), (4, 7, 1), (5, 8, 1), (7, 5, 1),
        (8, 11, 1), (9, 11, 1), (10, 8, 0), (11, 8, 0), (12, 10, 1), (13, 10, 1),
    )),
    (9, (
        (1, 9, 0), (2, 2, 0), (5, 8, 1), (6, 11, 0), (9, 12, 0), (10, 15, 0), (11, 8, 0),
        (12, 10, 1), (15, 9, 0),
    )),
    (1, (
        (0, 5, 1), (1, 3, 1), (2, 4, 1), (4, 13, 0), (5, 10, 0), (6, 12, 0), (7, 13, 0),
        (8, 14, 0), (9, 11, 0), (10, 13, 0), (13, 15, 0),
    )),
    (0, (
        (0, 9, 1), (2, 9, 1), (3, 9, 1), (4, 7, 0), (5, 7, 0), (6, 4, 0), (7, 4, 0),
        (12, 10, 0), (13, 10, 0),
    )),
    (7, (
        (1, 8, 1), (2, 2, 1), (8, 2, 1), (11, 8, 1), (12, 11, 1), (13, 11, 1), (14, 8, 0),
        (15, 8, 0),
    )),
    (1, (
        (1, 2, 0), (2, 9, 0), (3, 8, 0), (4, 10, 1), (5, 11, 0), (6, 8, 1), (7, 9, 0),
        (9, 15, 0), (10, 12, 0),
    )),
)


def partner(kind, chip):
    z, row = chip % 4, chip // 4
    if kind < 6:
        return chip ^ (4, 1, 8, 2, 3, 12)[kind]
    if z in (1, 2) and (kind - 6) >> (row % 2) & 1:
        return chip ^ 3
    return chip ^ 8


def grid_plan():
    ops = []
    for kind, sends in STEPS:
        sent = {source: (block, part) for source, block, part in sends}
        ops.append([(c, partner(kind, c), sent.get(c)) for c in range(16)])
    return ops, frozenset(range(12, 16))


def direct_plan(chips):
    ops = []
    for m in range(1, 9):
        for part in range(2 if m < 8 else 1):
            ops.append([(r + m, r, (r + m, part)) for r in range(chips - m)])
    return ops, frozenset()


def first_slot(k, core):
    return (k - core + ((core + k) & 1)) // 2


def left_tiles(block, part, chip, packed):
    m = block - chip
    ks = [2 * m + part] * 2
    if packed:
        ks = [2 * m, 2 * m + 1] if part == 0 else [NO_TERM, NO_TERM]
    return [k if m >= 0 and k < NO_TERM else NO_TERM for k in ks]


def by_chip(values, chip):
    if len(set(values)) == 1:
        return values[0]
    word = 0
    for at in range(0, len(values), 6):
        bits = sum(v << 5 * i for i, v in enumerate(values[at : at + 6]))
        word = jnp.where(chip >= at, bits, word)
    return (word >> 5 * (chip % 6)) & 31


def position():
    chip = lax.axis_index("row") * lax.axis_size("col") + lax.axis_index("col")
    return chip, lax.axis_index("depth")


VMEM = pl.BlockSpec(memory_space=pltpu.VMEM)
SMEM = pl.BlockSpec(memory_space=pltpu.SMEM)
HBM = pl.BlockSpec(memory_space=pltpu.HBM)
VMEM_LIMIT = 12 * 2**20
FIRST = 4
LAG = 4
ADD_AT = (9, 12, 16)
LAST = (2, 1)


def units_kernel(packed_from, choice_masks, fill_hbm, band_hbm, *refs):
    outs, flags, (fill_ref, band_ref, sems) = refs[:2], refs[2], refs[3:]
    fill_copy = pltpu.make_async_copy(fill_hbm, fill_ref, sems.at[2])
    copies = [
        pltpu.make_async_copy(band_hbm.at[row], band_ref.at[row], sems.at[row]) for row in range(2)
    ]
    for copy in (fill_copy, copies[1], copies[0]):
        copy.start()
    chip, core = position()
    for i, mask in enumerate(choice_masks):
        bit = ((mask >> chip) & 1).astype(jnp.float32)
        flags[i : i + 1, :] = jnp.full((1, flags.shape[1]), bit, flags.dtype)
    packed = chip >= packed_from
    fill_copy.wait()
    for part, unit in ((1, outs[1]), (0, outs[0])):
        copies[part].wait()
        for slot in range(SLOTS):
            row, t = part, slot
            if part == 0:
                row = jnp.where(packed, slot // 4, 0)
                t = jnp.where(packed, slot % 4, slot)
            entry = 2 * t + ((core + row) & 1)
            fill = fill_ref[row, entry].astype(jnp.float32)
            tile = band_ref[row, entry].astype(jnp.float32) * fill
            unit[:, slot * TILE : (slot + 1) * TILE] = tile.astype(jnp.bfloat16)


def add_terms(terms, left_ref, units, sums):
    width = SLOTS // 2 * TILE
    chip, core = position()
    for (first, second), unit in zip(terms, units):
        ks = [by_chip(first, chip), by_chip(second, chip)]
        slots = [first_slot(k, core) for k in ks]
        slots[1] = jnp.where(ks[0] == ks[1], slots[0] + SLOTS // 2, slots[1])
        for half, (k, slot) in enumerate(zip(ks, slots)):
            product = jnp.dot(
                left_ref[k],
                unit[:, half * width : (half + 1) * width],
                preferred_element_type=jnp.float32,
            )
            for q in range(SLOTS // 2):
                sums[slot + q] += product[:, q * TILE : (q + 1) * TILE]


def first_kernel(terms, reach_hbm, fill_hbm, band_hbm, *refs):
    units, (left, keep, token, sums) = refs[:2], refs[2:6]
    reach_ref, fill_ref, band_ref, sems = refs[6:]
    copies = [
        pltpu.make_async_copy(source, target, sems.at[i])
        for i, (source, target) in enumerate(
            [(reach_hbm, reach_ref), (fill_hbm, fill_ref), (band_hbm, band_ref)]
        )
    ]
    for copy in copies:
        copy.start()
    sums[...] = jnp.zeros(sums.shape, jnp.float32)
    for copy in copies:
        copy.wait()
    token[...] = jnp.zeros(token.shape, token.dtype)
    _, core = position()
    for row in range(2):
        for s in range(OUT_BAND // 2):
            kept = 2 * s + ((core + row) & 1) < reach_ref[row]
            value = jnp.where(kept, 1.0, 0.0).astype(jnp.float32)
            keep[row, s : s + 1, :] = jnp.full((1, TILE), value, jnp.float32)
    zero = jnp.zeros((TILE, TILE), jnp.bfloat16)
    left[0, TILE:] = zero
    left[16, :TILE] = zero
    left[NO_TERM] = jnp.zeros((2 * TILE, TILE), jnp.bfloat16)
    for row in range(2):
        for entry in range(16):
            fill = fill_ref[row, entry].astype(jnp.float32)
            tile = band_ref[row, entry].astype(jnp.float32) * fill
            left[entry + row, row * TILE : (row + 1) * TILE] = tile.astype(jnp.bfloat16)
    add_terms(terms, left, units, sums)


def more_kernel(terms, left_ref, after_ref, *refs):
    units, sums = refs[: len(terms)], refs[-1]
    for token in refs[len(terms) + 1 : -1]:
        token[...] = jnp.zeros(token.shape, token.dtype)
    add_terms(terms, left_ref, units, sums)


def last_kernel(terms, left_ref, keep_ref, *refs):
    units, kept, given, sums = refs[:-4], refs[-3], refs[-2], refs[-1]
    add_terms(terms, left_ref, units, sums)
    _, core = position()
    half = TILE // 2
    for row in range(2):
        shift = 0 if row == 0 else 1 - core
        for s in range(OUT_BAND // 2):
            keep = keep_ref[row, s : s + 1, :] > 0.5
            for out, side in ((kept, core), (given, 1 - core)):
                start = pl.multiple_of(row * TILE + side * half, half)
                tile = sums[s + shift, pl.ds(start, half), :]
                out[row, s] = jnp.where(keep, tile, 0.0).astype(jnp.bfloat16)


def place_kernel(partner, tiles, *refs):
    out, sems = refs[-2:]
    _, core = position()
    copies = []
    for row in range(2):
        odd = (core + row + partner) & 1
        copies.append(pltpu.make_async_copy(tiles.at[row], out.at[row, :, odd], sems.at[row]))
    for copy in copies:
        copy.start()
    for copy in copies:
        copy.wait()


def lookup(plan, chips):
    ops, packed = plan
    held = {"n0": [(r, 0) for r in range(chips)], "n1": [(r, 1) for r in range(chips)]}
    order = ["n0", "n1"] + list(range(len(ops)))
    picks = np.zeros((chips, len(ops)), np.int32)
    choices = []
    for o, moves in enumerate(ops):
        names = []
        got = [None] * chips
        for source, target, unit in moves:
            if unit is None:
                continue
            name = next(n for n in order if n in held and held[n][source] == unit)
            if name not in names:
                names.append(name)
            picks[source, o] = names.index(name)
            got[target] = unit
        held[o] = got
        choices.append(names)
    terms = {n: [[], []] for n in order}
    for r in range(chips):
        done = set()
        for n in order:
            unit = held[n][r]
            fresh = unit is not None and unit not in done
            done.add(unit)
            ks = left_tiles(*unit, r, unit[0] in packed) if fresh else [NO_TERM] * 2
            for half in range(2):
                terms[n][half].append(ks[half])
    if not packed:
        terms = {n: [[max(k, key=k.count)] for k in ks] for n, ks in terms.items()}
    return terms, picks, choices


def per_device(plan, chips, a_band, a_fill, c_reach):
    ops, packed = plan
    terms, picks, choices = lookup(plan, chips)
    reach = pltpu.with_memory_space_constraint(c_reach, pltpu.HBM)
    fill = pltpu.with_memory_space_constraint(a_fill, pltpu.HBM)
    band = pltpu.with_memory_space_constraint(a_band, pltpu.HBM)
    params = pltpu.CompilerParams(vmem_limit_bytes=VMEM_LIMIT)
    unit_shape = jax.ShapeDtypeStruct((TILE, SLOTS * TILE), jnp.bfloat16)
    token_shape = jax.ShapeDtypeStruct((1, SLOTS * TILE), jnp.float32)
    sums_shape = jax.ShapeDtypeStruct((SUMS, 2 * TILE, TILE), jnp.float32)
    choice_masks, flag_at = [], {}
    for o, names in enumerate(choices):
        flag_at[o] = len(choice_masks)
        for i in range(len(names) - 1):
            choice_masks.append(sum(int(picks[r, o] == i) << r for r in range(chips)))
    flags_shape = jax.ShapeDtypeStruct((max(8, len(choice_masks)), SLOTS * TILE), jnp.float32)
    n0, n1, flags = pl.pallas_call(
        functools.partial(units_kernel, min(packed, default=chips), choice_masks),
        out_shape=(unit_shape, unit_shape, flags_shape),
        in_specs=[HBM, HBM],
        out_specs=(VMEM,) * 3,
        scratch_shapes=[
            pltpu.SMEM(a_fill.shape, a_fill.dtype),
            pltpu.VMEM(a_band.shape, a_band.dtype),
            pltpu.SemaphoreType.DMA((3,)),
        ],
        compiler_params=params,
        name="units",
    )(fill, band)
    buffers = {"n0": n0, "n1": n1}
    payload = left = keep = sums = None
    added = 0

    def start():
        return pl.pallas_call(
            functools.partial(first_kernel, [terms["n0"], terms["n1"]]),
            out_shape=(
                jax.ShapeDtypeStruct((NO_TERM + 1, 2 * TILE, TILE), jnp.bfloat16),
                jax.ShapeDtypeStruct((2, OUT_BAND // 2, TILE), jnp.float32),
                token_shape,
                sums_shape,
            ),
            in_specs=[HBM, HBM, HBM, VMEM, VMEM],
            out_specs=(VMEM,) * 4,
            scratch_shapes=[
                pltpu.SMEM(c_reach.shape, c_reach.dtype),
                pltpu.SMEM(a_fill.shape, a_fill.dtype),
                pltpu.VMEM(a_band.shape, a_band.dtype),
                pltpu.SemaphoreType.DMA((3,)),
            ],
            compiler_params=params,
            name="first",
        )(reach, fill, band, n0, n1)

    def more(after, sums, names, tokens=1):
        units = [buffers[n] for n in names]
        return pl.pallas_call(
            functools.partial(more_kernel, [terms[n] for n in names]),
            out_shape=(token_shape,) * tokens + (sums_shape,),
            in_specs=[VMEM] * (3 + len(units)),
            out_specs=(VMEM,) * (tokens + 1),
            input_output_aliases={2 + len(units): tokens},
            compiler_params=params,
            name="more",
        )(left, after, *units, sums)

    for o, moves in enumerate(ops):
        sources = [buffers[n] for n in choices[o]]
        order = 0 * payload[:1].astype(jnp.float32) if o > 0 else 0
        if o == FIRST:
            left, keep, token, sums = start()
            order += token
        elif o in ADD_AT:
            token, sums = more(payload, sums, range(added, o - LAG))
            added = o - LAG
            order += token
        payload = sources[-1]
        if len(sources) == 1:
            payload = jnp.where(order > 0.5, n0, payload)
        for i in reversed(range(len(sources) - 1)):
            at = flag_at[o] + i
            payload = jnp.where(flags[at : at + 1] + order > 0.5, sources[i], payload)
        buffers[o] = lax.ppermute(payload, RC, [(s, t) for s, t, _ in moves])
    if sums is None:
        left, keep, _, sums = start()
    for count in LAST:
        (sums,) = more(buffers[added], sums, range(added, len(ops) - count), tokens=0)
        added = len(ops) - count

    piece = jax.ShapeDtypeStruct((2, OUT_BAND // 2, TILE // 2, TILE), jnp.bfloat16)
    units = [buffers[n] for n in range(added, len(ops))]
    n_in = 2 + len(units)
    kept, given, _ = pl.pallas_call(
        functools.partial(last_kernel, [terms[n] for n in range(added, len(ops))]),
        out_shape=(piece, piece, sums_shape),
        in_specs=[VMEM] * (n_in + 1),
        out_specs=(VMEM, VMEM, VMEM),
        input_output_aliases={n_in: 2},
        compiler_params=params,
        name="last",
    )(left, keep, *units, sums)
    taken = lax.ppermute(given, "depth", [(0, 1), (1, 0)])
    out = None
    for partner, tiles in enumerate((kept, taken)):
        out = pl.pallas_call(
            functools.partial(place_kernel, partner),
            out_shape=jax.ShapeDtypeStruct(
                (2, OUT_BAND // 2, 2, TILE // 2, TILE), jnp.bfloat16
            ),
            in_specs=[VMEM, HBM][: 1 + partner],
            out_specs=HBM,
            scratch_shapes=[pltpu.SemaphoreType.DMA((2,))],
            input_output_aliases={1: 0} if partner else {},
            compiler_params=params,
            name="place",
        )(*[tiles, out][: 1 + partner])
    return out.reshape(2, OUT_BAND, TILE // 2, TILE)


def solution(mesh):
    rows, cols = mesh.shape["row"], mesh.shape["col"]
    plan = grid_plan() if (rows, cols) == (4, 4) else direct_plan(rows * cols)
    in_specs = (P(RC, None, None, None), P(RC, None), P(RC))
    out_specs = P(RC, None, "depth", None)
    return jax.shard_map(
        functools.partial(per_device, plan, rows * cols),
        mesh=mesh,
        in_specs=in_specs,
        out_specs=out_specs,
        check_vma=False,
    )
```

```python
import functools

import jax
import jax.numpy as jnp
import numpy as np
from jax import lax
from jax.experimental import pallas as pl
from jax.experimental.pallas import tpu as pltpu
from jax.sharding import PartitionSpec as P

OUT_BAND = 24
TILE = 128
SLOTS = 8
SUMS = 17
NO_TERM = 17
RC = ("row", "col")


STEPS = (
    (1, (
        (1, 1, 0), (3, 3, 1), (4, 4, 1), (5, 5, 1), (6, 6, 1), (7, 7, 1), (8, 8, 0), (9, 9, 0),
        (10, 10, 1), (11, 11, 1), (13, 13, 0), (14, 14, 0), (15, 15, 0),
    )),
    (0, (
        (2, 2, 0), (4, 4, 0), (5, 5, 0), (6, 6, 0), (7, 7, 1), (8, 8, 1), (9, 9, 0),
        (10, 10, 1), (11, 11, 1), (12, 12, 0), (14, 14, 0), (15, 15, 0),
    )),
    (8, (
        (2, 2, 1), (4, 4, 1), (5, 5, 1), (6, 6, 1), (8, 8, 0), (9, 9, 1), (10, 10, 0),
        (11, 11, 0), (12, 12, 0), (13, 13, 0), (14, 14, 0), (15, 15, 0),
    )),
    (1, (
        (1, 1, 1), (3, 3, 0), (4, 4, 0), (5, 5, 0), (6, 6, 0), (7, 7, 0), (8, 8, 1), (9, 9, 1),
        (10, 10, 0), (11, 11, 0),
    )),
    (0, (
        (2, 3, 1), (4, 5, 1), (5, 4, 1), (6, 6, 1), (7, 6, 1), (8, 9, 0), (10, 10, 0),
        (12, 13, 0), (14, 15, 0), (15, 14, 0),
    )),
    (9, (
        (1, 5, 0), (2, 6, 0), (5, 4, 1), (6, 7, 1), (8, 9, 0), (9, 8, 0), (10, 11, 1),
        (11, 10, 1), (12, 8, 1), (13, 9, 0), (14, 10, 1), (15, 14, 0),
    )),
    (1, (
        (0, 8, 0), (1, 5, 0), (3, 11, 0), (4, 12, 0), (5, 6, 1), (8, 12, 0), (13, 14, 0),
        (14, 13, 0),
    )),
    (0, (
        (0, 8, 0), (1, 9, 1), (2, 10, 0), (3, 11, 0), (4, 4, 1), (5, 6, 1), (6, 7, 1),
        (7, 7, 0), (11, 10, 0), (12, 4, 1), (13, 13, 0), (14, 13, 0),
    )),
    (9, (
        (1, 9, 1), (2, 3, 0), (4, 5, 0), (5, 4, 0), (6, 7, 0), (8, 9, 1), (9, 8, 1),
        (10, 2, 1), (11, 10, 0), (12, 9, 0), (14, 10, 0), (15, 11, 1),
    )),
    (1, (
        (0, 9, 0), (1, 6, 0), (2, 5, 0), (3, 10, 1), (4, 8, 1), (5, 7, 1), (6, 5, 1),
        (7, 14, 0), (9, 11, 1), (10, 8, 0), (13, 10, 1), (14, 9, 0),
    )),
    (0, (
        (1, 6, 0), (2, 11, 0), (3, 10, 1), (4, 6, 1), (5, 7, 1), (6, 5, 1), (7, 6, 0),
        (12, 14, 0), (14, 9, 0),
    )),
    (9, (
        (1, 4, 1), (2, 3, 1), (5, 12, 0), (6, 10, 0), (10, 11, 0), (12, 13, 0), (14, 15, 0),
        (15, 13, 0),
    )),
    (1, (
        (0, 4, 0), (1, 3, 0), (2, 9, 1), (3, 7, 0), (4, 9, 0), (5, 7, 0), (6, 4, 0),
        (7, 11, 1), (9, 2, 1), (10, 8, 1), (13, 10, 0),
    )),
    (0, (
        (0, 6, 0), (1, 8, 0), (2, 10, 1), (3, 10, 0), (4, 7, 1), (5, 8, 1), (7, 5, 1),
        (8, 11, 1), (9, 11, 1), (10, 8, 0), (11, 8, 0), (12, 10, 1), (13, 10, 1),
    )),
    (9, (
        (1, 9, 0), (2, 2, 0), (5, 8, 1), (6, 11, 0), (9, 12, 0), (10, 15, 0), (11, 8, 0),
        (12, 10, 1), (15, 9, 0),
    )),
    (1, (
        (0, 5, 1), (1, 3, 1), (2, 4, 1), (4, 13, 0), (5, 10, 0), (6, 12, 0), (7, 13, 0),
        (8, 14, 0), (9, 11, 0), (10, 13, 0), (13, 15, 0),
    )),
    (0, (
        (0, 9, 1), (2, 9, 1), (3, 9, 1), (4, 7, 0), (5, 7, 0), (6, 4, 0), (7, 4, 0),
        (12, 10, 0), (13, 10, 0),
    )),
    (7, (
        (1, 8, 1), (2, 2, 1), (8, 2, 1), (11, 8, 1), (12, 11, 1), (13, 11, 1), (14, 8, 0),
        (15, 8, 0),
    )),
    (1, (
        (1, 2, 0), (2, 9, 0), (3, 8, 0), (4, 10, 1), (5, 11, 0), (6, 8, 1), (7, 9, 0),
        (9, 15, 0), (10, 12, 0),
    )),
)


def partner(kind, chip):
    z, row = chip % 4, chip // 4
    if kind < 6:
        return chip ^ (4, 1, 8, 2, 3, 12)[kind]
    if z in (1, 2) and (kind - 6) >> (row % 2) & 1:
        return chip ^ 3
    return chip ^ 8


def grid_plan():
    ops = []
    for kind, sends in STEPS:
        sent = {source: (block, part) for source, block, part in sends}
        ops.append([(c, partner(kind, c), sent.get(c)) for c in range(16)])
    return ops, frozenset(range(12, 16))


def direct_plan(chips):
    ops = []
    for m in range(1, 9):
        for part in range(2 if m < 8 else 1):
            ops.append([(r + m, r, (r + m, part)) for r in range(chips - m)])
    return ops, frozenset()


def first_slot(k, core):
    return (k - core + ((core + k) & 1)) // 2


def left_tiles(block, part, chip, packed):
    m = block - chip
    ks = [2 * m + part] * 2
    if packed:
        ks = [2 * m, 2 * m + 1] if part == 0 else [NO_TERM, NO_TERM]
    return [k if m >= 0 and k < NO_TERM else NO_TERM for k in ks]


def by_chip(values, chip):
    if len(set(values)) == 1:
        return values[0]
    word = 0
    for at in range(0, len(values), 6):
        bits = sum(v << 5 * i for i, v in enumerate(values[at : at + 6]))
        word = jnp.where(chip >= at, bits, word)
    return (word >> 5 * (chip % 6)) & 31


def position():
    chip = lax.axis_index("row") * lax.axis_size("col") + lax.axis_index("col")
    return chip, lax.axis_index("depth")


VMEM = pl.BlockSpec(memory_space=pltpu.VMEM)
SMEM = pl.BlockSpec(memory_space=pltpu.SMEM)
HBM = pl.BlockSpec(memory_space=pltpu.HBM)
VMEM_LIMIT = 12 * 2**20
FIRST = 4
LAG = 4
ADD_AT = (9, 12, 15)
LAST = (2, 1)


def units_kernel(packed_from, choice_masks, fill_hbm, band_hbm, *refs):
    outs, flags, (fill_ref, band_ref, sems) = refs[:2], refs[2], refs[3:]
    fill_copy = pltpu.make_async_copy(fill_hbm, fill_ref, sems.at[2])
    copies = [
        pltpu.make_async_copy(band_hbm.at[row], band_ref.at[row], sems.at[row]) for row in range(2)
    ]
    for copy in (fill_copy, *copies):
        copy.start()
    chip, core = position()
    for i, mask in enumerate(choice_masks):
        bit = ((mask >> chip) & 1).astype(jnp.float32)
        flags[i : i + 1, :] = jnp.full((1, flags.shape[1]), bit, flags.dtype)
    packed = chip >= packed_from
    for copy in (fill_copy, *copies):
        copy.wait()
    for part, unit in enumerate(outs):
        for slot in range(SLOTS):
            row, t = part, slot
            if part == 0:
                row = jnp.where(packed, slot // 4, 0)
                t = jnp.where(packed, slot % 4, slot)
            entry = 2 * t + ((core + row) & 1)
            fill = fill_ref[row, entry].astype(jnp.float32)
            tile = band_ref[row, entry].astype(jnp.float32) * fill
            unit[:, slot * TILE : (slot + 1) * TILE] = tile.astype(jnp.bfloat16)


def add_terms(terms, left_ref, units, sums):
    width = SLOTS // 2 * TILE
    chip, core = position()
    for (first, second), unit in zip(terms, units):
        ks = [by_chip(first, chip), by_chip(second, chip)]
        slots = [first_slot(k, core) for k in ks]
        slots[1] = jnp.where(ks[0] == ks[1], slots[0] + SLOTS // 2, slots[1])
        for half, (k, slot) in enumerate(zip(ks, slots)):
            product = jnp.dot(
                left_ref[k],
                unit[:, half * width : (half + 1) * width],
                preferred_element_type=jnp.float32,
            )
            for q in range(SLOTS // 2):
                sums[slot + q] += product[:, q * TILE : (q + 1) * TILE]


def first_kernel(terms, reach_hbm, fill_hbm, band_hbm, *refs):
    units, (left, keep, token, sums) = refs[:2], refs[2:6]
    reach_ref, fill_ref, band_ref, sems = refs[6:]
    copies = [
        pltpu.make_async_copy(source, target, sems.at[i])
        for i, (source, target) in enumerate(
            [(reach_hbm, reach_ref), (fill_hbm, fill_ref), (band_hbm, band_ref)]
        )
    ]
    for copy in copies:
        copy.start()
    sums[...] = jnp.zeros(sums.shape, jnp.float32)
    for copy in copies:
        copy.wait()
    token[...] = jnp.zeros(token.shape, token.dtype)
    _, core = position()
    for row in range(2):
        for s in range(OUT_BAND // 2):
            kept = 2 * s + ((core + row) & 1) < reach_ref[row]
            value = jnp.where(kept, 1.0, 0.0).astype(jnp.float32)
            keep[row, s : s + 1, :] = jnp.full((1, TILE), value, jnp.float32)
    zero = jnp.zeros((TILE, TILE), jnp.bfloat16)
    left[0, TILE:] = zero
    left[16, :TILE] = zero
    left[NO_TERM] = jnp.zeros((2 * TILE, TILE), jnp.bfloat16)
    for row in range(2):
        for entry in range(16):
            fill = fill_ref[row, entry].astype(jnp.float32)
            tile = band_ref[row, entry].astype(jnp.float32) * fill
            left[entry + row, row * TILE : (row + 1) * TILE] = tile.astype(jnp.bfloat16)
    add_terms(terms, left, units, sums)


def more_kernel(terms, left_ref, after_ref, *refs):
    units, sums = refs[: len(terms)], refs[-1]
    for token in refs[len(terms) + 1 : -1]:
        token[...] = jnp.zeros(token.shape, token.dtype)
    add_terms(terms, left_ref, units, sums)


def last_kernel(terms, left_ref, keep_ref, *refs):
    units, kept, given, sums = refs[:-4], refs[-3], refs[-2], refs[-1]
    add_terms(terms, left_ref, units, sums)
    _, core = position()
    half = TILE // 2
    for row in range(2):
        shift = 0 if row == 0 else 1 - core
        for s in range(OUT_BAND // 2):
            keep = keep_ref[row, s : s + 1, :] > 0.5
            for out, side in ((kept, core), (given, 1 - core)):
                start = pl.multiple_of(row * TILE + side * half, half)
                tile = sums[s + shift, pl.ds(start, half), :]
                out[row, s] = jnp.where(keep, tile, 0.0).astype(jnp.bfloat16)


def place_kernel(partner, tiles, *refs):
    out, sems = refs[-2:]
    _, core = position()
    copies = []
    for row in range(2):
        odd = (core + row + partner) & 1
        copies.append(pltpu.make_async_copy(tiles.at[row], out.at[row, :, odd], sems.at[row]))
    for copy in copies:
        copy.start()
    for copy in copies:
        copy.wait()


def lookup(plan, chips):
    ops, packed = plan
    held = {"n0": [(r, 0) for r in range(chips)], "n1": [(r, 1) for r in range(chips)]}
    order = ["n0", "n1"] + list(range(len(ops)))
    picks = np.zeros((chips, len(ops)), np.int32)
    choices = []
    for o, moves in enumerate(ops):
        names = []
        got = [None] * chips
        for source, target, unit in moves:
            if unit is None:
                continue
            name = next(n for n in order if n in held and held[n][source] == unit)
            if name not in names:
                names.append(name)
            picks[source, o] = names.index(name)
            got[target] = unit
        held[o] = got
        choices.append(names)
    terms = {n: [[], []] for n in order}
    for r in range(chips):
        done = set()
        for n in order:
            unit = held[n][r]
            fresh = unit is not None and unit not in done
            done.add(unit)
            ks = left_tiles(*unit, r, unit[0] in packed) if fresh else [NO_TERM] * 2
            for half in range(2):
                terms[n][half].append(ks[half])
    if not packed:
        terms = {n: [[max(k, key=k.count)] for k in ks] for n, ks in terms.items()}
    return terms, picks, choices


def per_device(plan, chips, a_band, a_fill, c_reach):
    ops, packed = plan
    terms, picks, choices = lookup(plan, chips)
    reach = pltpu.with_memory_space_constraint(c_reach, pltpu.HBM)
    fill = pltpu.with_memory_space_constraint(a_fill, pltpu.HBM)
    band = pltpu.with_memory_space_constraint(a_band, pltpu.HBM)
    params = pltpu.CompilerParams(vmem_limit_bytes=VMEM_LIMIT)
    unit_shape = jax.ShapeDtypeStruct((TILE, SLOTS * TILE), jnp.bfloat16)
    token_shape = jax.ShapeDtypeStruct((1, SLOTS * TILE), jnp.float32)
    sums_shape = jax.ShapeDtypeStruct((SUMS, 2 * TILE, TILE), jnp.float32)
    choice_masks, flag_at = [], {}
    for o, names in enumerate(choices):
        flag_at[o] = len(choice_masks)
        for i in range(len(names) - 1):
            choice_masks.append(sum(int(picks[r, o] == i) << r for r in range(chips)))
    flags_shape = jax.ShapeDtypeStruct((max(8, len(choice_masks)), SLOTS * TILE), jnp.float32)
    n0, n1, flags = pl.pallas_call(
        functools.partial(units_kernel, min(packed, default=chips), choice_masks),
        out_shape=(unit_shape, unit_shape, flags_shape),
        in_specs=[HBM, HBM],
        out_specs=(VMEM,) * 3,
        scratch_shapes=[
            pltpu.SMEM(a_fill.shape, a_fill.dtype),
            pltpu.VMEM(a_band.shape, a_band.dtype),
            pltpu.SemaphoreType.DMA((3,)),
        ],
        compiler_params=params,
        name="units",
    )(fill, band)
    buffers = {"n0": n0, "n1": n1}
    payload = left = keep = sums = None
    added = 0

    def start():
        return pl.pallas_call(
            functools.partial(first_kernel, [terms["n0"], terms["n1"]]),
            out_shape=(
                jax.ShapeDtypeStruct((NO_TERM + 1, 2 * TILE, TILE), jnp.bfloat16),
                jax.ShapeDtypeStruct((2, OUT_BAND // 2, TILE), jnp.float32),
                token_shape,
                sums_shape,
            ),
            in_specs=[HBM, HBM, HBM, VMEM, VMEM],
            out_specs=(VMEM,) * 4,
            scratch_shapes=[
                pltpu.SMEM(c_reach.shape, c_reach.dtype),
                pltpu.SMEM(a_fill.shape, a_fill.dtype),
                pltpu.VMEM(a_band.shape, a_band.dtype),
                pltpu.SemaphoreType.DMA((3,)),
            ],
            compiler_params=params,
            name="first",
        )(reach, fill, band, n0, n1)

    def more(after, sums, names, tokens=1):
        units = [buffers[n] for n in names]
        return pl.pallas_call(
            functools.partial(more_kernel, [terms[n] for n in names]),
            out_shape=(token_shape,) * tokens + (sums_shape,),
            in_specs=[VMEM] * (3 + len(units)),
            out_specs=(VMEM,) * (tokens + 1),
            input_output_aliases={2 + len(units): tokens},
            compiler_params=params,
            name="more",
        )(left, after, *units, sums)

    for o, moves in enumerate(ops):
        sources = [buffers[n] for n in choices[o]]
        order = 0 * payload[:1].astype(jnp.float32) if o > 0 else 0
        if o == FIRST:
            left, keep, token, sums = start()
            order += token
        elif o in ADD_AT:
            token, sums = more(payload, sums, range(added, o - LAG))
            added = o - LAG
            order += token
        payload = sources[-1]
        if len(sources) == 1:
            payload = jnp.where(order > 0.5, n0, payload)
        for i in reversed(range(len(sources) - 1)):
            at = flag_at[o] + i
            payload = jnp.where(flags[at : at + 1] + order > 0.5, sources[i], payload)
        buffers[o] = lax.ppermute(payload, RC, [(s, t) for s, t, _ in moves])
    if sums is None:
        left, keep, _, sums = start()
    for count in LAST:
        (sums,) = more(buffers[added], sums, range(added, len(ops) - count), tokens=0)
        added = len(ops) - count

    piece = jax.ShapeDtypeStruct((2, OUT_BAND // 2, TILE // 2, TILE), jnp.bfloat16)
    units = [buffers[n] for n in range(added, len(ops))]
    n_in = 2 + len(units)
    kept, given, _ = pl.pallas_call(
        functools.partial(last_kernel, [terms[n] for n in range(added, len(ops))]),
        out_shape=(piece, piece, sums_shape),
        in_specs=[VMEM] * (n_in + 1),
        out_specs=(VMEM, VMEM, VMEM),
        input_output_aliases={n_in: 2},
        compiler_params=params,
        name="last",
    )(left, keep, *units, sums)
    taken = lax.ppermute(given, "depth", [(0, 1), (1, 0)])
    out = None
    for partner, tiles in enumerate((kept, taken)):
        out = pl.pallas_call(
            functools.partial(place_kernel, partner),
            out_shape=jax.ShapeDtypeStruct(
                (2, OUT_BAND // 2, 2, TILE // 2, TILE), jnp.bfloat16
            ),
            in_specs=[VMEM, HBM][: 1 + partner],
            out_specs=HBM,
            scratch_shapes=[pltpu.SemaphoreType.DMA((2,))],
            input_output_aliases={1: 0} if partner else {},
            compiler_params=params,
            name="place",
        )(*[tiles, out][: 1 + partner])
    return out.reshape(2, OUT_BAND, TILE // 2, TILE)


def solution(mesh):
    rows, cols = mesh.shape["row"], mesh.shape["col"]
    plan = grid_plan() if (rows, cols) == (4, 4) else direct_plan(rows * cols)
    in_specs = (P(RC, None, None, None), P(RC, None), P(RC))
    out_specs = P(RC, None, "depth", None)
    return jax.shard_map(
        functools.partial(per_device, plan, rows * cols),
        mesh=mesh,
        in_specs=in_specs,
        out_specs=out_specs,
        check_vma=False,
    )
```
